32 devices in a mesh: groups: 2 (over x), inner: 16 (over z, y, core).
Axes of the slice: x: 2, y: 2, z: 4, core: 2. Of those that a mesh axis runs over, the one named last changes fastest.
Arguments:
- hidden_rows: bfloat16 [2048, 2048], P(('groups', 'inner')), parts along dimension 0, may hold values from -6 to 6
- token_embed: bfloat16 [2048, 2048], P(('groups', 'inner')), parts along dimension 0, may hold values from -6 to 6
- first_routes: int32 [2048, 8], P(('groups', 'inner')), parts along dimension 0, may hold values from 0 to 15, all different within a row; in each aligned block of 64 rows (0 to 63, 64 to 127, ...) at most 48 rows name the same one
- first_gates: float32 [2048, 8], P(('groups', 'inner')), parts along dimension 0, may hold values from 0.2 to 0.6
- first_gate_up: bfloat16 [16, 2048, 1024], P('inner'), may hold values from -0.125 to 0.125
- first_down: bfloat16 [16, 512, 2048], P('inner'), may hold values from -0.25 to 0.25
- second_routes: int32 [2048, 8], P(('groups', 'inner')), parts along dimension 0, may hold values from 0 to 15, all different within a row; in each aligned block of 64 rows (0 to 63, 64 to 127, ...) at most 48 rows name the same one
- second_gates: float32 [2048, 8], P(('groups', 'inner')), parts along dimension 0, may hold values from 0.2 to 0.6
- second_gate_up: bfloat16 [16, 2048, 1024], P('inner'), may hold values from -0.125 to 0.125
- second_down: bfloat16 [16, 512, 2048], P('inner'), may hold values from -0.25 to 0.25
- hidden_gain: float32 [2048], replicated, may hold values from 0.25 to 1.75
- embed_gain: float32 [2048], replicated, may hold values from 0.25 to 1.75
- merge_weight: bfloat16 [4096, 2048], P('inner'), may hold values from -0.09375 to 0.09375
Outputs:
- final_rows: bfloat16 [2048, 2048], P(('groups', 'inner')), parts along dimension 0
The draws below stay inside these ranges and needn't reach their ends.
There are 2 independent parts, one for each index of `groups`. The reference program is written for one: setup_inputs(seed, part) draws one part's arguments, and reference() takes and returns one part's arrays. A program takes and returns all parts, laid end to end along the dimension named above; an argument that names none is the same for every part. Nothing has to cross between parts.
Inputs may be any that keep to these rules, and one draw needn't show every extreme that they name: `first_routes`: among the 64 tokens of one block, no expert is named more than 48 times, and in every draw some expert is named exactly 48 times in some block. `second_routes`: among the 64 tokens of one block, no expert is named more than 48 times, and in every draw some expert is named exactly 48 times in some block.
All inputs are finite; a program needn't handle non-finite values.
Results may differ from the reference program's by a relative error of at most 0.01.
Values may be sent and summed in bfloat16 or wider, within the bound.
A program may use at most 128 MiB of HBM per device.

```python
import math
import jax
import jax.numpy as jnp
import numpy as np
from jax import lax

D = 2048
FFW = 512
TOP = 8
TOK_DEV = 64
EXPERTS = 16
TOKENS = 1024
CAP = 48
N_INNER = 16


def block_scale(key, extent, pieces, low, top_value):
    def one(axis_at, blocks):
        steps = jax.random.uniform(jax.random.fold_in(jax.random.fold_in(key, 6), axis_at), (blocks,), jnp.float32, low / len(pieces), top_value / len(pieces))
        return jnp.repeat(jnp.exp(steps), extent[axis_at] // blocks).reshape((-1,) + (1,) * (len(extent) - axis_at - 1))

    loudness = one(*pieces[0])
    for cut in pieces[1:]:
        loudness = loudness * one(*cut)
    return loudness


def deal_out(rng, own, number, rows, count, top, most, skew):
    order = jax.random.permutation(rng, count)
    heavy_load, usual = shares(count, rows * top, most, skew, True), shares(count, rows * top, most, skew, False)
    places = jnp.arange(count)

    def named(tallies, turn):
        used = int((tallies > 0).sum())
        fixed = max(1, used // 4)
        passed = fixed + (places - fixed + turn * (used - fixed)) % max(1, count - fixed)
        return jnp.zeros((count,), jnp.int32).at[order[jnp.where(places < fixed, places, passed)]].set(jnp.asarray(tallies, jnp.int32))

    tallies = jnp.where(number % 4 == 0, named(heavy_load, number // 4), named(usual, number - number // 4 - 1))
    mixed = jax.random.permutation(jax.random.fold_in(own, 3), count)
    giver, receiver = mixed[0:count // 2 * 2:2], mixed[1:count // 2 * 2:2]
    slack = jnp.minimum(tallies[giver] - 1, most - tallies[receiver]) // 2
    slack = jnp.where((giver == order[0]) | (receiver == order[0]) | (tallies[receiver] == 0), 0, jnp.maximum(slack, 0))
    passed = jax.random.randint(jax.random.fold_in(own, 4), (count // 2,), 0, 1 << 20) % (slack + 1)
    tallies = tallies.at[giver].add(-passed).at[receiver].add(passed)
    labels = jnp.searchsorted(jnp.cumsum(tallies), jnp.arange(rows * top), side="right").astype(jnp.int32)
    listing = labels.reshape(top, rows).T
    listing = listing[jax.random.permutation(jax.random.fold_in(own, 1), rows)]
    turn = jax.random.randint(jax.random.fold_in(own, 2), (rows, 1), 0, top)
    return jnp.take_along_axis(listing, (jnp.arange(top)[None, :] + turn) % top, axis=1)


def shares(amount, total, limit, slope, full):
    weights = [(1 << 20) // math.isqrt(rank ** slope) + 1 for rank in range(1, amount + 1)]
    largest = limit if full else min(limit, max(-(-total // amount), total * weights[0] // sum(weights)))
    least = 1 if total - largest >= amount - 1 else 0
    holding, spare = [largest] + [least] * (amount - 1), total - largest - least * (amount - 1)
    while spare > 0:
        candidates = [i for i in range(1, amount) if holding[i] < largest] or [i for i in range(1, amount) if holding[i] < limit]
        whole, budget = sum([weights[i] for i in candidates]), spare
        for i in candidates:
            more = min(limit - holding[i], max(1, budget * weights[i] // whole), spare)
            holding[i] = holding[i] + more
            spare = spare - more
    return np.array(holding)


def bell_draw(own_key, extent, spread, reach, cuts=(), held_as=jnp.bfloat16):
    values = jax.random.normal(own_key, extent, jnp.float32) * spread
    if len(cuts) > 0:
        values = block_scale(own_key, extent, cuts, -0.22, 0.18) * values
    return jnp.clip(values, min=-reach, max=reach).astype(held_as)


def setup_inputs(seed: int = 0, part: int = 0) -> dict:
    key_of = jax.random.split(jax.random.key(seed), 14)
    part_splits = jax.random.split(jax.random.fold_in(key_of[13], part), 14)
    hidden_rows = bell_draw(part_splits[0], (TOKENS, D), 1.0, 6.0, ((0, 16),))
    token_embed = bell_draw(part_splits[1], (TOKENS, D), 1.0, 6.0, ((0, 16),))
    first_routes_keys = jax.random.split(jax.random.fold_in(part_splits[2], 1), TOKENS // TOK_DEV)
    first_routes_turns = jax.random.permutation(jax.random.fold_in(part_splits[2], 3), TOKENS // TOK_DEV)
    first_routes = jax.vmap(lambda own, number: deal_out(jax.random.fold_in(part_splits[2], 2), own, number, TOK_DEV, EXPERTS, TOP, CAP, 2))(first_routes_keys, first_routes_turns).reshape((TOKENS, TOP))
    first_gates = jnp.clip(0.2 + 0.400000021 * jax.random.uniform(part_splits[3], (TOKENS, TOP), jnp.float32) ** block_scale(part_splits[3], (TOKENS, TOP), ((0, 16),), -0.2, 0.2), 0.2, 0.6)
    first_gate_up = bell_draw(key_of[4], (EXPERTS, D, 2 * FFW), D ** -0.5, 0.125, ((0, 16),))
    first_down = bell_draw(key_of[5], (EXPERTS, FFW, D), FFW ** -0.5, 0.25, ((0, 16),))
    second_routes_keys = jax.random.split(jax.random.fold_in(part_splits[6], 1), TOKENS // TOK_DEV)
    second_routes_turns = jax.random.permutation(jax.random.fold_in(part_splits[6], 3), TOKENS // TOK_DEV)
    second_routes = jax.vmap(lambda own, number: deal_out(jax.random.fold_in(part_splits[6], 2), own, number, TOK_DEV, EXPERTS, TOP, CAP, 1))(second_routes_keys, second_routes_turns).reshape((TOKENS, TOP))
    second_gates = jnp.clip(0.2 + 0.400000021 * jax.random.uniform(part_splits[7], (TOKENS, TOP), jnp.float32) ** block_scale(part_splits[7], (TOKENS, TOP), ((0, 16),), -0.2, 0.2), 0.2, 0.6)
    second_gate_up = bell_draw(key_of[8], (EXPERTS, D, 2 * FFW), D ** -0.5, 0.125, ((0, 16),))
    second_down = bell_draw(key_of[9], (EXPERTS, FFW, D), FFW ** -0.5, 0.25, ((0, 16),))
    hidden_gain = jnp.clip(1.0 + 0.15 * jax.random.normal(key_of[10], (D,), jnp.float32), 0.25, 1.75)
    embed_gain = jnp.clip(1.0 + 0.15 * jax.random.normal(key_of[11], (D,), jnp.float32), 0.25, 1.75)
    merge_weight = bell_draw(key_of[12], (2 * D, D), (2 * D) ** -0.5, 0.09375, ((0, 16),))
    return dict(hidden_rows=hidden_rows, token_embed=token_embed, first_routes=first_routes, first_gates=first_gates, first_gate_up=first_gate_up, first_down=first_down, second_routes=second_routes, second_gates=second_gates, second_gate_up=second_gate_up, second_down=second_down, hidden_gain=hidden_gain, embed_gain=embed_gain, merge_weight=merge_weight)


EPSILON = 1e-06

def expert_apply(slot_rows, expert_gu, expert_down):
    inner_width = expert_down.shape[0]
    projected = jnp.dot(slot_rows, expert_gu, preferred_element_type=jnp.float32)
    inner = (jax.nn.silu(projected[:, :inner_width]) * projected[:, inner_width:]).astype(jnp.bfloat16)
    return jnp.dot(inner, expert_down, preferred_element_type=jnp.float32).astype(jnp.bfloat16)

def rms_scale(values, gain_vec):
    widened = values.astype(jnp.float32)
    inverse_rms = lax.rsqrt(lax.optimization_barrier(jnp.mean(widened * widened, axis=-1, keepdims=True)) + EPSILON)
    return (widened * inverse_rms * gain_vec.astype(jnp.float32)).astype(jnp.bfloat16)

def routed_reference(inputs, routes, weights_in, gate_up, down_proj):
    tokens_all, feature_dim = inputs.shape
    top_count = routes.shape[1]
    experts = gate_up.shape[0]
    blocks = N_INNER
    per_block = tokens_all // blocks
    capacity = max(2, 3 * per_block * top_count // (2 * experts))
    grouped = routes.reshape(blocks, per_block * top_count)
    onehot = (grouped[:, :, None] == jnp.arange(experts, dtype=jnp.int32)[None, None, :]).astype(jnp.int32)
    ranking = lax.optimization_barrier(jnp.sum(onehot * (jnp.cumsum(onehot, axis=1) - 1), axis=2))
    source = jnp.arange(blocks, dtype=jnp.int32)[:, None] * capacity
    position = (grouped * (blocks * capacity) + source + ranking).reshape(-1).astype(jnp.int32)
    repeated = jnp.repeat(inputs, top_count, axis=0)
    buffer_rows = jnp.zeros((experts * blocks * capacity, feature_dim), jnp.bfloat16).at[position].set(repeated)

    def one_expert(operands):
        slot_rows, expert_gu, expert_down = operands
        return expert_apply(slot_rows, expert_gu, expert_down)
    outputs = lax.map(one_expert, (buffer_rows.reshape(experts, blocks * capacity, feature_dim), gate_up, down_proj))
    picked = outputs.reshape(-1, feature_dim)[position].reshape(tokens_all, top_count, feature_dim)
    return lax.optimization_barrier(jnp.sum(picked.astype(jnp.float32) * weights_in.astype(jnp.float32)[:, :, None], axis=1))

def reference(hidden_rows, token_embed, first_routes, first_gates, first_gate_up, first_down, second_routes, second_gates, second_gate_up, second_down, hidden_gain, embed_gain, merge_weight):
    first_moe = routed_reference(hidden_rows, first_routes, first_gates, first_gate_up, first_down)
    after_first = (hidden_rows.astype(jnp.float32) + first_moe).astype(jnp.bfloat16)
    merged_in = jnp.concatenate([rms_scale(after_first, hidden_gain), rms_scale(token_embed, embed_gain)], axis=1)
    merged = jnp.dot(merged_in, merge_weight, preferred_element_type=jnp.float32)
    after_merge = (after_first.astype(jnp.float32) + jax.nn.silu(merged)).astype(jnp.bfloat16)
    second_moe = routed_reference(after_merge, second_routes, second_gates, second_gate_up, second_down)
    return (after_merge.astype(jnp.float32) + second_moe).astype(jnp.bfloat16)
```

```python
import functools

import jax
import jax.numpy as jnp
from jax import lax
from jax.experimental import pallas as pl
from jax.experimental.pallas import tpu as pltpu
from jax.sharding import PartitionSpec as P

EPSILON = 1e-06
LANES = 128
CUTS = 2
VMEM_LIMIT = 60 * 1024 * 1024


class Ring:
    def __init__(self, devices, tok):
        self.devices, self.tok = devices, tok
        self.chips = devices // 2
        self.reach = self.chips // 2
        self.rise = self.chips // 2
        me = lax.axis_index("inner")
        chip = me // 2
        across = chip % 2
        along = chip // 2
        self.core = me % 2
        self.place = along * (1 - across) + (2 * self.rise - 1 - along) * across
        self.me = me
        self.spans = [(0, 0)]
        for distance in range(1, self.reach):
            self.spans += [(distance, 0), (distance, 1)]
        self.spans.append((self.reach, 0))

    def device(self, shift, other):
        place = (self.place + shift + self.chips) % self.chips
        across = place // self.rise
        along = place * (1 - across) + (2 * self.rise - 1 - place) * across
        core = self.core * (1 - other) + (1 - self.core) * other
        return (along * 2 + across) * 2 + core

    def first(self, distance, s):
        if distance == 0:
            return ((self.reach - 1) * 4 + 2) * self.tok
        return ((distance - 1) * 4 + 2 * s) * self.tok

    def rows(self, distance, s):
        return pl.ds(self.first(distance, s), 2 * self.tok)

    def side(self, distance, s, other):
        return pl.ds(self.first(distance, s) + other * self.tok, self.tok)

    def half(self, way, distance, other, k):
        part = self.tok // 2
        if distance == 0:
            s, column = 0, k
        elif distance == self.reach:
            s, column = 0, k
        else:
            s, column = (0 if k == way else 1), way
        return pl.ds(self.first(distance, s) + other * self.tok + column * part, part)

    def slot(self, way, distance, other):
        if distance == 0:
            return (self.reach - 1) * 4 + 2 + other
        if distance == self.reach:
            return (self.reach - 1) * 4 + other
        return (distance - 1) * 4 + way * 2 + other


def remote(src, dst, send, recv, device):
    return pltpu.make_async_remote_copy(
        src_ref=src, dst_ref=dst, send_sem=send, recv_sem=recv,
        device_id={"inner": device}, device_id_type=pl.DeviceIdType.MESH,
    )


def wide(values):
    return values.astype(jnp.float32)


def narrow(values):
    return values.astype(jnp.bfloat16)


class Reduce:
    def __init__(self, ring, bufs, started):
        self.ring, self.started = ring, started
        (self.share, self.paired, self.arrived, self.pair_send, self.pair_recv, self.send,
         self.recv) = bufs
        self.cut = self.share.shape[1] // CUTS

    def pair_copy(self, distance, s):
        ring = self.ring
        slot = ring.spans.index((distance, s))
        here = self.paired.at[pl.ds(slot * ring.tok, ring.tok)]
        return remote(
            self.share.at[ring.side(distance, s, 1)], here,
            self.pair_send.at[slot], self.pair_recv.at[slot], ring.device(0, 1),
        ), here

    def begin(self, copy):
        copy.start()
        self.started.append(copy)

    def start_pair(self, distance, s):
        self.begin(self.pair_copy(distance, s)[0])

    def finish_pair(self, distance, s):
        copy, here = self.pair_copy(distance, s)
        copy.wait_recv()
        rows = self.ring.side(distance, s, 0)
        self.share[rows, :] = narrow(wide(self.share[rows, :]) + wide(here[...]))

    def columns(self, c):
        return pl.ds(c * self.cut, self.cut)

    def hop(self, way, distance, k, c):
        ring = self.ring
        rows = ring.tok // 2
        slot = (way * ring.reach + distance - 1) * 2 + k
        landing = self.arrived.at[pl.ds(slot * rows, rows), self.columns(c)]
        return remote(
            self.share.at[ring.half(1 - way, distance, 0, k), self.columns(c)], landing,
            self.send.at[slot * CUTS + c], self.recv.at[slot * CUTS + c],
            ring.device(1 - 2 * way, 0),
        ), landing

    def launch(self, distance, flip):
        for c in range(CUTS):
            for way in (0, 1):
                self.begin(self.hop(way, distance, 1 - way if flip else way, c)[0])

    def step(self, distance, flip):
        for c in range(CUTS):
            for way in (0, 1):
                k = 1 - way if flip else way
                copy, landing = self.hop(way, distance + 1, k, c)
                copy.wait_recv()
                at = (self.ring.half(1 - way, distance, 0, k), self.columns(c))
                self.share[at] = narrow(wide(self.share[at]) + wide(landing[...]))
                self.begin(self.hop(way, distance, k, c)[0])

    def total(self):
        parts = []
        for c in range(CUTS):
            halves = []
            for k in (0, 1):
                piece = wide(self.share[self.ring.half(0, 0, 0, k), self.columns(c)])
                for way in (0, 1):
                    copy, landing = self.hop(way, 1, k, c)
                    copy.wait_recv()
                    piece = piece + wide(landing[...])
                halves.append(piece)
            parts.append(jnp.concatenate(halves, axis=0))
        return jnp.concatenate(parts, axis=1)


def reduce_scratch(devices, tok, width):
    reach = devices // 4
    return [
        pltpu.VMEM((devices * tok, width), jnp.bfloat16),
        pltpu.VMEM((2 * reach * tok, width), jnp.bfloat16),
        pltpu.VMEM((2 * reach * tok, width), jnp.bfloat16),
        pltpu.SemaphoreType.DMA((2 * reach,)),
        pltpu.SemaphoreType.DMA((2 * reach,)),
        pltpu.SemaphoreType.DMA((4 * reach * CUTS,)),
        pltpu.SemaphoreType.DMA((4 * reach * CUTS,)),
    ]


def gather_scratch(devices, tok, width):
    reach = devices // 4
    return [
        pltpu.VMEM((devices * tok, width), jnp.bfloat16),
        pltpu.SemaphoreType.DMA((4 * reach,)),
        pltpu.SemaphoreType.DMA((4 * reach,)),
        pltpu.SemaphoreType.DMA((4 * reach + 1,)),
        pltpu.SemaphoreType.DMA((4 * reach + 1,)),
    ]


def normed(values, gain):
    widened = wide(values)
    inverse_rms = lax.rsqrt(jnp.mean(widened * widened, axis=-1, keepdims=True) + EPSILON)
    return narrow(widened * inverse_rms * gain)


def gate_lanes(devices, turned, tables):
    rows = tables[0][0].shape[1]
    turned[...] = jnp.zeros_like(turned)
    for layer, (routes, gates) in enumerate(tables):
        base = 2 * layer * devices
        expert = lax.broadcasted_iota(jnp.int32, (devices, rows), 0)
        dense = jnp.zeros((devices, rows), jnp.float32)
        for k in range(routes.shape[0]):
            dense = dense + jnp.where(expert == routes[k : k + 1, :], gates[k : k + 1, :], 0.0)
        high = wide(narrow(dense))
        turned[base : base + devices, :rows] = high
        turned[base + devices : base + 2 * devices, :rows] = dense - high
    return narrow(turned[...].T[:rows, :])


def block_kernel(devices, *refs):
    (routes1, gates1, routes2, gates2, hidden_gain, embed_gain, hidden_ref, embed_ref,
     gu1_ref, down1_ref, weight_ref, gu2_ref, down2_ref, out_ref) = refs[:14]
    scratch = list(refs[14:])
    take = lambda count: [scratch.pop(0) for _ in range(count)]
    gu1, down1, weight, gu2, down2, load_sem = take(6)
    turned, embed, after_first, pieces, landed, inner = take(6)
    piece_send, piece_recv, own_sem, lane_send, lane_pair = take(5)
    gather1, gather2 = take(5), take(5)
    reduce1, reduce2, reduce3 = take(7), take(7), take(7)
    tok, width = hidden_ref.shape
    hidden = down1.shape[0]
    depth = weight.shape[0]
    lanes = gather1[0].shape[1] - width
    ring = Ring(devices, tok)
    reach = ring.reach
    part = tok // 2

    barrier = pltpu.get_barrier_semaphore()
    neighbours = [ring.device(1, 0), ring.device(-1, 0), ring.device(0, 1)]
    for device in neighbours:
        pl.semaphore_signal(
            barrier, inc=1, device_id={"inner": device}, device_id_type=pl.DeviceIdType.MESH
        )
    own_rows = ring.side(0, 0, 0)
    loads = [
        pltpu.make_async_copy(source, target, load_sem.at[i])
        for i, (source, target) in enumerate(
            [(hidden_ref, gather1[0].at[own_rows, pl.ds(0, width)]), (embed_ref, embed),
             (gu1_ref.at[0], gu1), (down1_ref.at[0], down1), (weight_ref, weight),
             (gu2_ref.at[0], gu2), (down2_ref.at[0], down2)]
        )
    ]
    waiting = list(range(len(loads)))

    def need(*which):
        for i in which:
            if i in waiting:
                waiting.remove(i)
                loads[i].wait()

    pl.semaphore_wait(barrier, len(neighbours))
    started = []

    def begin(copy):
        copy.start()
        started.append(copy)

    partners = [(0, 0, 1)]
    for distance in range(1, reach + 1):
        for other in (0, 1):
            partners.append((0, distance, other))
            if distance < reach:
                partners.append((1, distance, other))

    def streams(s):
        return [(way, 1 - way if s else way) for way in (0, 1)]

    def ring_copy(bufs, way, distance, k):
        everyone, send, recv = bufs[:3]
        slot = (way * reach + distance - 1) * 2 + k
        if distance == 1:
            origin = everyone.at[ring.half(way, 0, 0, k)]
        else:
            origin = everyone.at[ring.half(way, distance - 1, 0, k)]
        return remote(
            origin, everyone.at[ring.half(way, distance, 0, k)], send.at[slot], recv.at[slot],
            ring.device(1 - 2 * way, 0),
        )

    def sibling_copy(bufs, way, distance, k):
        everyone, sib_send, sib_recv = bufs[0], bufs[3], bufs[4]
        if distance == 0:
            slot, origin, landing = 4 * reach, own_rows, ring.side(0, 0, 1)
        else:
            slot = (way * reach + distance - 1) * 2 + k
            origin, landing = ring.half(way, distance, 0, k), ring.half(way, distance, 1, k)
        return remote(
            everyone.at[origin], everyone.at[landing], sib_send.at[slot], sib_recv.at[slot],
            ring.device(0, 1),
        )

    def first_sends():
        everyone, send, recv, sib_send, sib_recv = gather1
        narrow_cut, lane_cut = pl.ds(0, width), pl.ds(width, lanes)

        def send_rows(way, k):
            slot = way * reach * 2 + k
            return remote(
                hidden_ref.at[pl.ds(k * part, part)],
                everyone.at[ring.half(way, 1, 0, k), narrow_cut],
                send.at[slot], recv.at[slot], ring.device(1 - 2 * way, 0),
            )

        def send_lanes(way, k):
            slot = way * reach * 2 + k
            return remote(
                everyone.at[ring.half(way, 0, 0, k), lane_cut],
                everyone.at[ring.half(way, 1, 0, k), lane_cut],
                lane_send.at[way * 2 + k], recv.at[slot], ring.device(1 - 2 * way, 0),
            )

        for way, k in streams(0):
            begin(send_rows(way, k))
        begin(remote(
            hidden_ref, everyone.at[ring.side(0, 0, 1), narrow_cut],
            sib_send.at[4 * reach], sib_recv.at[4 * reach], ring.device(0, 1),
        ))
        for load in loads:
            load.start()
        everyone[own_rows, lane_cut] = gate_lanes(
            devices, turned, [(routes1[...], gates1[...]), (routes2[...], gates2[...])]
        )
        for way, k in streams(0):
            begin(send_lanes(way, k))
        begin(remote(
            everyone.at[own_rows, lane_cut], everyone.at[ring.side(0, 0, 1), lane_cut],
            lane_pair.at[0], sib_recv.at[4 * reach], ring.device(0, 1),
        ))
        for way, k in streams(1):
            begin(send_rows(way, k))
            begin(send_lanes(way, k))

    def layer(bufs, first, reducing, load_ids, gu, down, meanwhile):
        everyone = bufs[0]
        share = reducing.share
        gate_rows = gather1[0]
        step = min(256, hidden)
        steps = hidden // step

        def pass_on(distance, s):
            for way, k in streams(s):
                ring_copy(bufs, way, distance, k).wait_recv()
                if distance + 1 < reach or (distance + 1 == reach and s == 0):
                    begin(ring_copy(bufs, way, distance + 1, k))
                begin(sibling_copy(bufs, way, distance, k))

        def from_sibling(distance, s):
            if distance == 0:
                sibling_copy(bufs, 0, 0, 0).wait_recv()
            else:
                for way, k in streams(s):
                    sibling_copy(bufs, way, distance, k).wait_recv()

        def up(first_row, count, low, high):
            rows = pl.ds(first_row, count)

            @pl.loop(low, high)
            def _(j):
                left = pl.ds(pl.multiple_of(j * step, step), step)
                right = pl.ds(pl.multiple_of(hidden + j * step, step), step)
                x = everyone[rows, :width]
                g = jnp.dot(x, gu[:, left], preferred_element_type=jnp.float32)
                u = jnp.dot(x, gu[:, right], preferred_element_type=jnp.float32)
                inner[:count, left] = narrow(jax.nn.silu(g) * u)

        def finish(first_row, count, *spans):
            rows = pl.ds(first_row, count)
            lane = lax.broadcasted_iota(jnp.int32, (count, lanes), 1)
            mine = (lane == ring.me + first * devices) | (lane == ring.me + (first + 1) * devices)
            gate = jnp.sum(
                jnp.where(mine, wide(gate_rows[rows, width:]), 0.0), axis=1, keepdims=True
            )
            span = min(512, width)

            @pl.loop(0, width // span)
            def _(j):
                cut = pl.ds(pl.multiple_of(j * span, span), span)
                out = jnp.dot(
                    inner[:count, :], down[:, cut], preferred_element_type=jnp.float32
                )
                share[rows, cut] = narrow(out * gate)

            for at in spans:
                reducing.start_pair(*at)

        near = ring.first(0, 0)
        from_sibling(0, 0)
        need(load_ids[0])
        up(near, 2 * tok, 0, steps)
        need(load_ids[1])
        finish(near, 2 * tok, (0, 0))
        meanwhile()
        pass_on(1, 0)
        for distance in range(1, reach - 1):
            pass_on(distance, 1)
            from_sibling(distance, 0)
            from_sibling(distance, 1)
            up(ring.first(distance, 0), 4 * tok, 0, steps // 2)
            pass_on(distance + 1, 0)
            up(ring.first(distance, 0), 4 * tok, steps // 2, steps)
            finish(ring.first(distance, 0), 4 * tok, (distance, 0), (distance, 1))
            if distance == 1:
                reducing.finish_pair(0, 0)
            else:
                reducing.finish_pair(distance - 1, 0)
                reducing.finish_pair(distance - 1, 1)
        last = reach - 1
        pass_on(last, 1)
        from_sibling(last, 0)
        up(ring.first(last, 0), 2 * tok, 0, steps)
        finish(ring.first(last, 0), 2 * tok, (last, 0))
        pass_on(reach, 0)
        from_sibling(last, 1)
        reducing.finish_pair(last, 0)
        reducing.launch(last, True)
        from_sibling(reach, 0)
        up(ring.first(last, 1), 4 * tok, 0, steps)
        finish(ring.first(last, 1), 4 * tok, (reach, 0), (last, 1))
        reducing.finish_pair(last - 1, 0)
        reducing.finish_pair(last - 1, 1)
        reducing.step(last - 1, True)
        reducing.finish_pair(reach, 0)
        reducing.launch(reach, False)
        reducing.finish_pair(last, 1)
        for distance in range(last, 0, -1):
            if distance > 2:
                reducing.step(distance - 2, True)
            reducing.step(distance, False)

    def target_of(way, distance, other):
        return ring.device(distance * (1 - 2 * way), other)

    def piece(way, distance, other):
        target = target_of(way, distance, other)
        slot = ring.slot(way, distance, other)
        return remote(
            pieces.at[target], landed.at[pl.ds(slot * tok, tok)],
            piece_send.at[slot], piece_recv.at[slot], target,
        ), target * depth >= width

    def send_pieces(late):
        for partner in reversed(partners):
            copy, embedded = piece(*partner)

            @pl.when(embedded if late == 0 else jnp.logical_not(embedded))
            def _():
                copy.start()

            if late:
                started.append(copy)

    def merge(reducing):
        own = pltpu.make_async_copy(
            pieces.at[ring.me], landed.at[pl.ds(ring.slot(0, 0, 0) * tok, tok)], own_sem.at[0]
        )
        own.start()
        need(4)
        share = reducing.share
        came = set()

        def arrive(distance):
            if distance not in came:
                came.add(distance)
                for partner in partners:
                    if partner[1] == distance:
                        piece(*partner)[0].wait_recv()
                if distance == 0:
                    own.wait()

        def product(distance, s):
            arrive(distance)
            pick = []
            for other in (0, 1):
                for column in (0, 1):
                    if distance in (0, reach):
                        way, k = 0, column
                    else:
                        way, k = column, (column if s == 0 else 1 - column)
                    row = ring.slot(way, distance, other) * tok + k * part
                    pick.append(landed[row : row + part, :])
            x = jnp.concatenate(pick, axis=0)
            rows = ring.rows(distance, s)
            span = min(512, width)
            for j in range(width // span):
                cut = pl.ds(j * span, span)
                share[rows, cut] = narrow(
                    jnp.dot(x, weight[:, cut], preferred_element_type=jnp.float32)
                )
            reducing.start_pair(distance, s)

        last = reach - 1
        product(reach, 0)
        product(last, 0)
        reducing.finish_pair(reach, 0)
        reducing.launch(reach, False)
        product(last, 1)
        reducing.finish_pair(last, 0)
        reducing.launch(last, True)
        product(last - 1, 0)
        reducing.finish_pair(last, 1)
        for distance in range(last, 0, -1):
            if distance > 1:
                product(distance - 1, 1)
                reducing.finish_pair(distance - 1, 0)
            else:
                product(0, 0)
            reducing.step(distance, False)
            if distance > 1:
                if distance > 2:
                    product(distance - 2, 0)
                reducing.finish_pair(distance - 1, 1)
                reducing.step(distance - 1, True)
        reducing.finish_pair(0, 0)

    def scatter_pieces(values, at):
        for j in range(width // depth):
            pieces[at + j] = values[:, j * depth : (j + 1) * depth]

    def embed_pieces():
        need(1)
        scatter_pieces(normed(embed[...], embed_gain[...]), width // depth)

    first_sends()
    need(0)
    reducing = Reduce(ring, reduce1, started)
    layer(gather1, 0, reducing, (2, 3), gu1, down1, embed_pieces)
    send_pieces(0)
    first = narrow(wide(gather1[0][own_rows, :width]) + reducing.total())
    after_first[...] = first
    scatter_pieces(normed(first, hidden_gain[...]), 0)
    send_pieces(1)
    reducing = Reduce(ring, reduce2, started)
    merge(reducing)
    gather2[0][own_rows, :] = narrow(wide(after_first[...]) + jax.nn.silu(reducing.total()))
    for s in (0, 1):
        for way, k in streams(s):
            begin(ring_copy(gather2, way, 1, k))
        if s == 0:
            begin(sibling_copy(gather2, 0, 0, 0))
    reducing = Reduce(ring, reduce3, started)
    layer(gather2, 2, reducing, (5, 6), gu2, down2, lambda: None)
    out_ref[...] = narrow(wide(gather2[0][own_rows, :]) + reducing.total())
    for copy in started:
        copy.wait_send()


def fused(hidden_rows, token_embed, first_routes, first_gates, first_gate_up, first_down,
          second_routes, second_gates, second_gate_up, second_down, hidden_gain, embed_gain,
          merge_weight):
    devices = lax.axis_size("inner")
    tok, width = hidden_rows.shape
    hidden = first_down.shape[1]
    depth = merge_weight.shape[0]
    lanes = -(-4 * devices // LANES) * LANES
    vmem = pl.BlockSpec(memory_space=pltpu.VMEM)
    hbm = pl.BlockSpec(memory_space=pl.ANY)
    bf16 = jnp.bfloat16
    scratch = [
        pltpu.VMEM(first_gate_up.shape[1:], bf16),
        pltpu.VMEM(first_down.shape[1:], bf16),
        pltpu.VMEM(merge_weight.shape, bf16),
        pltpu.VMEM(second_gate_up.shape[1:], bf16),
        pltpu.VMEM(second_down.shape[1:], bf16),
        pltpu.SemaphoreType.DMA((7,)),
        pltpu.VMEM((lanes, -(-tok // LANES) * LANES), jnp.float32),
        pltpu.VMEM((tok, width), bf16),
        pltpu.VMEM((tok, width), bf16),
        pltpu.VMEM((devices, tok, depth), bf16),
        pltpu.VMEM((devices * tok, depth), bf16),
        pltpu.VMEM((4 * tok, hidden), bf16),
        pltpu.SemaphoreType.DMA((devices,)),
        pltpu.SemaphoreType.DMA((devices,)),
        pltpu.SemaphoreType.DMA((1,)),
        pltpu.SemaphoreType.DMA((4,)),
        pltpu.SemaphoreType.DMA((1,)),
    ]
    scratch += gather_scratch(devices, tok, width + lanes) + gather_scratch(devices, tok, width)
    for _ in range(3):
        scratch += reduce_scratch(devices, tok, width)
    return pl.pallas_call(
        functools.partial(block_kernel, devices),
        out_shape=jax.ShapeDtypeStruct((tok, width), bf16),
        in_specs=[vmem] * 6 + [hbm] * 7,
        out_specs=vmem,
        scratch_shapes=scratch,
        compiler_params=pltpu.CompilerParams(
            collective_id=0, has_side_effects=True, vmem_limit_bytes=VMEM_LIMIT
        ),
    )(first_routes.T, first_gates.T, second_routes.T, second_gates.T, hidden_gain[None],
      embed_gain[None], hidden_rows, token_embed, first_gate_up, first_down, merge_weight,
      second_gate_up, second_down)


def rms_scale(values, gain_vec):
    widened = values.astype(jnp.float32)
    inverse_rms = lax.rsqrt(jnp.mean(widened * widened, axis=-1, keepdims=True) + EPSILON)
    return (widened * inverse_rms * gain_vec).astype(jnp.bfloat16)


def dense_gates(routes, gates, experts):
    hit = routes[:, :, None] == jnp.arange(experts, dtype=jnp.int32)[None, None, :]
    return jnp.sum(jnp.where(hit, gates[:, :, None], 0.0), axis=1)


def plain_layer(devices, rows, routes, gates, gate_up, down):
    dense = lax.all_gather(dense_gates(routes, gates, devices), "inner", axis=0, tiled=True)
    column = lax.dynamic_slice_in_dim(dense, lax.axis_index("inner"), 1, axis=1)
    everyone = lax.all_gather(rows, "inner", axis=0, tiled=True)
    width = down.shape[1]
    projected = jnp.dot(everyone, gate_up[0], preferred_element_type=jnp.float32)
    inner = narrow(jax.nn.silu(projected[:, :width]) * projected[:, width:])
    share = narrow(jnp.dot(inner, down[0], preferred_element_type=jnp.float32) * column)
    total = lax.psum_scatter(share, "inner", scatter_dimension=0, tiled=True)
    return narrow(wide(rows) + wide(total))


def plain_merge(after_first, merged_in, weight):
    columns = lax.all_to_all(merged_in, "inner", split_axis=1, concat_axis=0, tiled=True)
    partial = narrow(jnp.dot(columns, weight, preferred_element_type=jnp.float32))
    merged = lax.psum_scatter(partial, "inner", scatter_dimension=0, tiled=True)
    return narrow(wide(after_first) + jax.nn.silu(wide(merged)))


def unfused(hidden_rows, token_embed, first_routes, first_gates, first_gate_up, first_down,
            second_routes, second_gates, second_gate_up, second_down, hidden_gain, embed_gain,
            merge_weight):
    devices = lax.axis_size("inner")
    after_first = plain_layer(
        devices, hidden_rows, first_routes, first_gates, first_gate_up, first_down
    )
    merged_in = jnp.concatenate(
        [rms_scale(after_first, hidden_gain), rms_scale(token_embed, embed_gain)], axis=1
    )
    after_merge = plain_merge(after_first, merged_in, merge_weight)
    return plain_layer(devices, after_merge, second_routes, second_gates, second_gate_up, second_down)


def local(hidden_rows, *others):
    devices = lax.axis_size("inner")
    tok, width = hidden_rows.shape
    fits = (
        12 * devices * tok * width * 2 <= VMEM_LIMIT
        and devices % 4 == 0 and devices >= 16 and tok % 32 == 0
    )
    return (fused if fits else unfused)(hidden_rows, *others)


def solution(mesh):
    rows = P(("groups", "inner"), None)
    return jax.shard_map(
        local,
        mesh=mesh,
        in_specs=(
            rows, rows, rows, rows,
            P("inner", None, None),
            P("inner", None, None),
            rows, rows,
            P("inner", None, None),
            P("inner", None, None),
            P(),
            P(),
            P("inner", None),
        ),
        out_specs=rows,
        check_vma=False,
    )
```

```python
import functools

import jax
import jax.numpy as jnp
from jax import lax
from jax.experimental import pallas as pl
from jax.experimental.pallas import tpu as pltpu
from jax.sharding import PartitionSpec as P

EPSILON = 1e-06
LANES = 128
CUTS = 4
VMEM_LIMIT = 60 * 1024 * 1024


class Ring:
    def __init__(self, devices, tok):
        self.devices, self.tok = devices, tok
        self.chips = devices // 2
        self.reach = self.chips // 2
        self.rise = self.chips // 2
        me = lax.axis_index("inner")
        chip = me // 2
        across = chip % 2
        along = chip // 2
        self.core = me % 2
        self.place = along * (1 - across) + (2 * self.rise - 1 - along) * across
        self.me = me
        self.spans = [(0, 0)]
        for distance in range(1, self.reach):
            self.spans += [(distance, 0), (distance, 1)]
        self.spans.append((self.reach, 0))

    def device(self, shift, other):
        place = (self.place + shift + self.chips) % self.chips
        across = place // self.rise
        along = place * (1 - across) + (2 * self.rise - 1 - place) * across
        core = self.core * (1 - other) + (1 - self.core) * other
        return (along * 2 + across) * 2 + core

    def first(self, distance, s):
        if distance == 0:
            return ((self.reach - 1) * 4 + 2) * self.tok
        return ((distance - 1) * 4 + 2 * s) * self.tok

    def rows(self, distance, s):
        return pl.ds(self.first(distance, s), 2 * self.tok)

    def side(self, distance, s, other):
        return pl.ds(self.first(distance, s) + other * self.tok, self.tok)

    def half(self, way, distance, other, k):
        part = self.tok // 2
        if distance == 0:
            s, column = 0, k
        elif distance == self.reach:
            s, column = 0, k
        else:
            s, column = (0 if k == way else 1), way
        return pl.ds(self.first(distance, s) + other * self.tok + column * part, part)

    def chunk(self, way, distance, k):
        if distance == self.reach:
            return way
        return 2 + (way * (self.reach - 1) + distance - 1) * 2 + k

    def slot(self, way, distance, other):
        if distance == 0:
            return (self.reach - 1) * 4 + 2 + other
        if distance == self.reach:
            return (self.reach - 1) * 4 + other
        return (distance - 1) * 4 + way * 2 + other


def remote(src, dst, send, recv, device):
    return pltpu.make_async_remote_copy(
        src_ref=src, dst_ref=dst, send_sem=send, recv_sem=recv,
        device_id={"inner": device}, device_id_type=pl.DeviceIdType.MESH,
    )


def wide(values):
    return values.astype(jnp.float32)


def narrow(values):
    return values.astype(jnp.bfloat16)


def sent(ring, whole, sem):
    remote(whole, whole, sem, sem, ring.device(0, 1)).wait_send()


class Reduce:
    def __init__(self, ring, bufs, recvs):
        self.ring = ring
        self.share, self.paired, self.arrived, self.send = bufs
        self.pair_recv, self.recv = recvs
        self.cut = self.share.shape[1] // CUTS

    def pair_copy(self, distance, s):
        ring = self.ring
        slot = ring.spans.index((distance, s))
        here = self.paired.at[pl.ds(slot * ring.tok, ring.tok)]
        return remote(
            self.share.at[ring.side(distance, s, 1)], here,
            self.send.at[0], self.pair_recv.at[slot], ring.device(0, 1),
        ), here

    def start_pair(self, distance, s):
        self.pair_copy(distance, s)[0].start()

    def finish_pair(self, distance, s):
        copy, here = self.pair_copy(distance, s)
        copy.wait_recv()
        rows = self.ring.side(distance, s, 0)
        self.share[rows, :] = narrow(wide(self.share[rows, :]) + wide(here[...]))

    def columns(self, c):
        return pl.ds(c * self.cut, self.cut)

    def hop(self, way, distance, k, c):
        ring = self.ring
        rows = ring.tok // 2
        slot = ring.chunk(way, distance, k)
        landing = self.arrived.at[pl.ds(slot * rows, rows), self.columns(c)]
        return remote(
            self.share.at[ring.half(1 - way, distance, 0, k), self.columns(c)], landing,
            self.send.at[1], self.recv.at[slot * CUTS + c],
            ring.device(1 - 2 * way, 0),
        ), landing

    def launch(self, distance, flip):
        for c in range(CUTS):
            for way in (0, 1):
                self.hop(way, distance, 1 - way if flip else way, c)[0].start()

    def step(self, distance, flip):
        for c in range(CUTS):
            for way in (0, 1):
                k = 1 - way if flip else way
                copy, landing = self.hop(way, distance + 1, k, c)
                copy.wait_recv()
                at = (self.ring.half(1 - way, distance, 0, k), self.columns(c))
                self.share[at] = narrow(wide(self.share[at]) + wide(landing[...]))
                self.hop(way, distance, k, c)[0].start()

    def drain(self):
        ring = self.ring
        sent(ring, self.share.at[pl.ds(0, 2 * ring.reach * ring.tok)], self.send.at[0])
        sent(ring, self.share.at[pl.ds(0, (2 * ring.reach - 1) * ring.tok)], self.send.at[1])

    def total(self):
        parts = []
        for c in range(CUTS):
            halves = []
            for k in (0, 1):
                piece = wide(self.share[self.ring.half(0, 0, 0, k), self.columns(c)])
                for way in (0, 1):
                    copy, landing = self.hop(way, 1, k, c)
                    copy.wait_recv()
                    piece = piece + wide(landing[...])
                halves.append(piece)
            parts.append(jnp.concatenate(halves, axis=0))
        return jnp.concatenate(parts, axis=1)


def reduce_scratch(devices, tok, width):
    reach = devices // 4
    return [
        pltpu.VMEM((devices * tok, width), jnp.bfloat16),
        pltpu.VMEM((2 * reach * tok, width), jnp.bfloat16),
        pltpu.VMEM(((2 * reach - 1) * tok, width), jnp.bfloat16),
        pltpu.SemaphoreType.DMA((2,)),
    ]


def reduce_recvs(devices):
    reach = devices // 4
    return [
        pltpu.SemaphoreType.DMA((2 * reach,)),
        pltpu.SemaphoreType.DMA(((4 * reach - 2) * CUTS,)),
    ]


def gather_scratch(devices, tok, width):
    return [
        pltpu.VMEM((devices * tok, width), jnp.bfloat16),
        pltpu.SemaphoreType.DMA((2,)),
    ]


def normed(values, gain):
    widened = wide(values)
    inverse_rms = lax.rsqrt(jnp.mean(widened * widened, axis=-1, keepdims=True) + EPSILON)
    return narrow(widened * inverse_rms * gain)


def gate_lanes(devices, turned, tables):
    rows = tables[0][0].shape[1]
    turned[...] = jnp.zeros_like(turned)
    for layer, (routes, gates) in enumerate(tables):
        base = 2 * layer * devices
        expert = lax.broadcasted_iota(jnp.int32, (devices, rows), 0)
        dense = jnp.zeros((devices, rows), jnp.float32)
        for k in range(routes.shape[0]):
            dense = dense + jnp.where(expert == routes[k : k + 1, :], gates[k : k + 1, :], 0.0)
        high = wide(narrow(dense))
        turned[base : base + devices, :rows] = high
        turned[base + devices : base + 2 * devices, :rows] = dense - high
    return narrow(turned[...].T[:rows, :])


def block_kernel(devices, *refs):
    (routes1, gates1, routes2, gates2, hidden_gain, embed_gain, hidden_ref, embed_ref,
     gu1_ref, down1_ref, weight_ref, gu2_ref, down2_ref, out_ref) = refs[:14]
    scratch = list(refs[14:])
    take = lambda count: [scratch.pop(0) for _ in range(count)]
    gu1, down1, weight, gu2, down2, load_sem = take(6)
    turned, embed, after_first, pieces, landed, inner = take(6)
    piece_send, piece_recv, own_sem, ring_recv, sib_recv = take(5)
    gather1, gather2 = take(2), take(2)
    reduce1, reduce2, reduce3 = take(4), take(4), take(4)
    recvs1, recvs2 = take(2), take(2)
    tok, width = hidden_ref.shape
    hidden = down1.shape[0]
    depth = weight.shape[0]
    lanes = gather1[0].shape[1] - width
    ring = Ring(devices, tok)
    reach = ring.reach
    part = tok // 2

    barrier = pltpu.get_barrier_semaphore()
    neighbours = [ring.device(1, 0), ring.device(-1, 0), ring.device(0, 1)]
    for device in neighbours:
        pl.semaphore_signal(
            barrier, inc=1, device_id={"inner": device}, device_id_type=pl.DeviceIdType.MESH
        )
    own_rows = ring.side(0, 0, 0)
    loads = [
        pltpu.make_async_copy(source, target, load_sem.at[i])
        for i, (source, target) in enumerate(
            [(hidden_ref, gather1[0].at[own_rows, pl.ds(0, width)]), (embed_ref, embed),
             (gu1_ref.at[0], gu1), (down1_ref.at[0], down1), (weight_ref, weight),
             (gu2_ref.at[0], gu2), (down2_ref.at[0], down2)]
        )
    ]
    waiting = list(range(len(loads)))

    def need(*which):
        for i in which:
            if i in waiting:
                waiting.remove(i)
                loads[i].wait()

    def begin(copy):
        copy.start()

    partners = [(0, 0, 1)]
    for distance in range(1, reach + 1):
        for other in (0, 1):
            partners.append((0, distance, other))
            if distance < reach:
                partners.append((1, distance, other))

    def streams(s):
        return [(way, 1 - way if s else way) for way in (0, 1)]

    def ring_copy(bufs, way, distance, k):
        everyone, send = bufs
        slot = ring.chunk(way, distance, k)
        if distance == 1:
            origin = everyone.at[ring.half(way, 0, 0, k)]
        else:
            origin = everyone.at[ring.half(way, distance - 1, 0, k)]
        return remote(
            origin, everyone.at[ring.half(way, distance, 0, k)], send.at[0], ring_recv.at[slot],
            ring.device(1 - 2 * way, 0),
        )

    def sibling_copy(bufs, way, distance, k):
        everyone, send = bufs
        if distance == 0:
            s, origin, landing = 0, own_rows, ring.side(0, 0, 1)
        else:
            s = 0 if distance == reach or k == way else 1
            origin, landing = ring.half(way, distance, 0, k), ring.half(way, distance, 1, k)
        return remote(
            everyone.at[origin], everyone.at[landing], send.at[1],
            sib_recv.at[ring.spans.index((distance, s))], ring.device(0, 1),
        )

    def first_sends():
        everyone, send = gather1
        narrow_cut, lane_cut = pl.ds(0, width), pl.ds(width, lanes)

        def send_rows(way, k):
            return remote(
                hidden_ref.at[pl.ds(k * part, part)],
                everyone.at[ring.half(way, 1, 0, k), narrow_cut],
                send.at[0], ring_recv.at[ring.chunk(way, 1, k)], ring.device(1 - 2 * way, 0),
            )

        def send_lanes(way, k):
            return remote(
                everyone.at[ring.half(way, 0, 0, k), lane_cut],
                everyone.at[ring.half(way, 1, 0, k), lane_cut],
                send.at[0], ring_recv.at[ring.chunk(way, 1, k)], ring.device(1 - 2 * way, 0),
            )

        for load in loads:
            load.start()
        everyone[own_rows, lane_cut] = gate_lanes(
            devices, turned, [(routes1[...], gates1[...]), (routes2[...], gates2[...])]
        )
        pl.semaphore_wait(barrier, len(neighbours))
        for way, k in streams(0):
            begin(send_rows(way, k))
            begin(send_lanes(way, k))
        begin(remote(
            hidden_ref, everyone.at[ring.side(0, 0, 1), narrow_cut],
            send.at[1], sib_recv.at[0], ring.device(0, 1),
        ))
        begin(remote(
            everyone.at[own_rows, lane_cut], everyone.at[ring.side(0, 0, 1), lane_cut],
            send.at[1], sib_recv.at[0], ring.device(0, 1),
        ))
        for way, k in streams(1):
            begin(send_rows(way, k))
            begin(send_lanes(way, k))

    def layer(bufs, first, reducing, load_ids, gu, down, meanwhile):
        everyone = bufs[0]
        share = reducing.share
        gate_rows = gather1[0]
        step = min(256, hidden)
        steps = hidden // step

        def pass_on(distance, s):
            for way, k in streams(s):
                ring_copy(bufs, way, distance, k).wait_recv()
                if distance + 1 < reach or (distance + 1 == reach and s == 0):
                    begin(ring_copy(bufs, way, distance + 1, k))
                begin(sibling_copy(bufs, way, distance, k))

        def from_sibling(distance, s):
            both = bufs[0].at[ring.side(distance, s, 1)]
            remote(
                both, both, bufs[1].at[1], sib_recv.at[ring.spans.index((distance, s))],
                ring.device(0, 1),
            ).wait_recv()

        def up(first_row, count, low, high):
            rows = pl.ds(first_row, count)

            @pl.loop(low, high)
            def _(j):
                left = pl.ds(pl.multiple_of(j * step, step), step)
                right = pl.ds(pl.multiple_of(hidden + j * step, step), step)
                x = everyone[rows, :width]
                g = jnp.dot(x, gu[:, left], preferred_element_type=jnp.float32)
                u = jnp.dot(x, gu[:, right], preferred_element_type=jnp.float32)
                inner[:count, left] = narrow(jax.nn.silu(g) * u)

        def finish(first_row, count, *spans):
            rows = pl.ds(first_row, count)
            lane = lax.broadcasted_iota(jnp.int32, (count, lanes), 1)
            mine = (lane == ring.me + first * devices) | (lane == ring.me + (first + 1) * devices)
            gate = jnp.sum(
                jnp.where(mine, wide(gate_rows[rows, width:]), 0.0), axis=1, keepdims=True
            )
            span = min(512, width)

            @pl.loop(0, width // span)
            def _(j):
                cut = pl.ds(pl.multiple_of(j * span, span), span)
                out = jnp.dot(
                    inner[:count, :], down[:, cut], preferred_element_type=jnp.float32
                )
                share[rows, cut] = narrow(out * gate)

            for at in spans:
                reducing.start_pair(*at)

        near = ring.first(0, 0)
        from_sibling(0, 0)
        need(load_ids[0])
        up(near, 2 * tok, 0, steps)
        need(load_ids[1])
        pass_on(1, 0)
        finish(near, 2 * tok, (0, 0))
        meanwhile()
        for distance in range(1, reach - 1):
            pass_on(distance, 1)
            from_sibling(distance, 0)
            from_sibling(distance, 1)
            up(ring.first(distance, 0), 4 * tok, 0, steps // 2)
            pass_on(distance + 1, 0)
            up(ring.first(distance, 0), 4 * tok, steps // 2, steps)
            finish(ring.first(distance, 0), 4 * tok, (distance, 0), (distance, 1))
            if distance == 1:
                reducing.finish_pair(0, 0)
            else:
                reducing.finish_pair(distance - 1, 0)
                reducing.finish_pair(distance - 1, 1)
        last = reach - 1
        pass_on(last, 1)
        from_sibling(last, 0)
        up(ring.first(last, 0), 2 * tok, 0, steps)
        finish(ring.first(last, 0), 2 * tok, (last, 0))
        pass_on(reach, 0)
        from_sibling(last, 1)
        reducing.finish_pair(last, 0)
        reducing.launch(last, True)
        from_sibling(reach, 0)
        up(ring.first(last, 1), 4 * tok, 0, steps)
        finish(ring.first(last, 1), 4 * tok, (reach, 0), (last, 1))
        reducing.finish_pair(last - 1, 0)
        reducing.finish_pair(last - 1, 1)
        reducing.step(last - 1, True)
        reducing.finish_pair(reach, 0)
        reducing.launch(reach, False)
        reducing.finish_pair(last, 1)
        for distance in range(last, 0, -1):
            if distance > 2:
                reducing.step(distance - 2, True)
            reducing.step(distance, False)

    def target_of(way, distance, other):
        return ring.device(distance * (1 - 2 * way), other)

    def piece(way, distance, other):
        target = target_of(way, distance, other)
        slot = ring.slot(way, distance, other)
        return remote(
            pieces.at[target], landed.at[pl.ds(slot * tok, tok)],
            piece_send.at[0], piece_recv.at[distance], target,
        ), target * depth >= width

    def send_pieces(late):
        for partner in reversed(partners):
            copy, embedded = piece(*partner)

            @pl.when(embedded if late == 0 else jnp.logical_not(embedded))
            def _():
                copy.start()

    def merge(reducing):
        own = pltpu.make_async_copy(
            pieces.at[ring.me], landed.at[pl.ds(ring.slot(0, 0, 0) * tok, tok)], own_sem.at[0]
        )
        own.start()
        need(4)
        share = reducing.share
        came = set()

        def arrive(distance):
            if distance not in came:
                came.add(distance)
                low = min(ring.slot(*p) for p in partners if p[1] == distance)
                count = sum(p[1] == distance for p in partners)
                whole = landed.at[pl.ds(low * tok, count * tok)]
                remote(
                    whole, whole, piece_send.at[0], piece_recv.at[distance], ring.device(0, 1)
                ).wait_recv()
                if distance == 0:
                    own.wait()

        def product(distance, s):
            arrive(distance)
            pick = []
            for other in (0, 1):
                for column in (0, 1):
                    if distance in (0, reach):
                        way, k = 0, column
                    else:
                        way, k = column, (column if s == 0 else 1 - column)
                    row = ring.slot(way, distance, other) * tok + k * part
                    pick.append(landed[row : row + part, :])
            x = jnp.concatenate(pick, axis=0)
            rows = ring.rows(distance, s)
            span = min(512, width)
            for j in range(width // span):
                cut = pl.ds(j * span, span)
                share[rows, cut] = narrow(
                    jnp.dot(x, weight[:, cut], preferred_element_type=jnp.float32)
                )
            reducing.start_pair(distance, s)

        last = reach - 1
        product(reach, 0)
        product(last, 0)
        reducing.finish_pair(reach, 0)
        reducing.launch(reach, False)
        product(last, 1)
        reducing.finish_pair(last, 0)
        reducing.launch(last, True)
        product(last - 1, 0)
        reducing.finish_pair(last, 1)
        for distance in range(last, 0, -1):
            if distance > 1:
                product(distance - 1, 1)
                reducing.finish_pair(distance - 1, 0)
            else:
                product(0, 0)
            reducing.step(distance, False)
            if distance > 1:
                if distance > 2:
                    product(distance - 2, 0)
                reducing.finish_pair(distance - 1, 1)
                reducing.step(distance - 1, True)
        reducing.finish_pair(0, 0)

    def scatter_pieces(values, at):
        for j in range(width // depth):
            pieces[at + j] = values[:, j * depth : (j + 1) * depth]

    def embed_pieces():
        need(1)
        scatter_pieces(normed(embed[...], embed_gain[...]), width // depth)

    first_sends()
    need(0)
    reducing1 = reducing = Reduce(ring, reduce1, recvs1)
    layer(gather1, 0, reducing, (2, 3), gu1, down1, embed_pieces)
    send_pieces(0)
    first = narrow(wide(gather1[0][own_rows, :width]) + reducing.total())
    after_first[...] = first
    scatter_pieces(normed(first, hidden_gain[...]), 0)
    send_pieces(1)
    reducing2 = reducing = Reduce(ring, reduce2, recvs2)
    merge(reducing)
    gather2[0][own_rows, :] = narrow(wide(after_first[...]) + jax.nn.silu(reducing.total()))
    for s in (0, 1):
        for way, k in streams(s):
            begin(ring_copy(gather2, way, 1, k))
        if s == 0:
            begin(sibling_copy(gather2, 0, 0, 0))
    reducing3 = reducing = Reduce(ring, reduce3, recvs2)
    layer(gather2, 2, reducing, (5, 6), gu2, down2, lambda: None)
    out_ref[...] = narrow(wide(gather2[0][own_rows, :]) + reducing.total())
    for everyone, send in (gather1, gather2):
        sent(ring, everyone.at[pl.ds(0, (2 * reach - 1) * tok)], send.at[0])
        sent(ring, everyone.at[pl.ds(0, 2 * reach * tok)], send.at[1])
    sent(ring, landed.at[pl.ds(0, (devices - 1) * tok)], piece_send.at[0])
    for each in (reducing1, reducing2, reducing3):
        each.drain()


def fused(hidden_rows, token_embed, first_routes, first_gates, first_gate_up, first_down,
          second_routes, second_gates, second_gate_up, second_down, hidden_gain, embed_gain,
          merge_weight):
    devices = lax.axis_size("inner")
    tok, width = hidden_rows.shape
    hidden = first_down.shape[1]
    depth = merge_weight.shape[0]
    lanes = -(-4 * devices // LANES) * LANES
    reach = devices // 4
    vmem = pl.BlockSpec(memory_space=pltpu.VMEM)
    hbm = pl.BlockSpec(memory_space=pl.ANY)
    bf16 = jnp.bfloat16
    scratch = [
        pltpu.VMEM(first_gate_up.shape[1:], bf16),
        pltpu.VMEM(first_down.shape[1:], bf16),
        pltpu.VMEM(merge_weight.shape, bf16),
        pltpu.VMEM(second_gate_up.shape[1:], bf16),
        pltpu.VMEM(second_down.shape[1:], bf16),
        pltpu.SemaphoreType.DMA((7,)),
        pltpu.VMEM((lanes, -(-tok // LANES) * LANES), jnp.float32),
        pltpu.VMEM((tok, width), bf16),
        pltpu.VMEM((tok, width), bf16),
        pltpu.VMEM((devices, tok, depth), bf16),
        pltpu.VMEM((devices * tok, depth), bf16),
        pltpu.VMEM((4 * tok, hidden), bf16),
        pltpu.SemaphoreType.DMA((1,)),
        pltpu.SemaphoreType.DMA((reach + 1,)),
        pltpu.SemaphoreType.DMA((1,)),
        pltpu.SemaphoreType.DMA((4 * reach - 2,)),
        pltpu.SemaphoreType.DMA((2 * reach,)),
    ]
    scratch += gather_scratch(devices, tok, width + lanes) + gather_scratch(devices, tok, width)
    for _ in range(3):
        scratch += reduce_scratch(devices, tok, width)
    scratch += reduce_recvs(devices) + reduce_recvs(devices)
    return pl.pallas_call(
        functools.partial(block_kernel, devices),
        out_shape=jax.ShapeDtypeStruct((tok, width), bf16),
        in_specs=[vmem] * 6 + [hbm] * 7,
        out_specs=vmem,
        scratch_shapes=scratch,
        compiler_params=pltpu.CompilerParams(
            collective_id=0, has_side_effects=True, vmem_limit_bytes=VMEM_LIMIT
        ),
    )(first_routes.T, first_gates.T, second_routes.T, second_gates.T, hidden_gain[None],
      embed_gain[None], hidden_rows, token_embed, first_gate_up, first_down, merge_weight,
      second_gate_up, second_down)


def rms_scale(values, gain_vec):
    widened = values.astype(jnp.float32)
    inverse_rms = lax.rsqrt(jnp.mean(widened * widened, axis=-1, keepdims=True) + EPSILON)
    return (widened * inverse_rms * gain_vec).astype(jnp.bfloat16)


def dense_gates(routes, gates, experts):
    hit = routes[:, :, None] == jnp.arange(experts, dtype=jnp.int32)[None, None, :]
    return jnp.sum(jnp.where(hit, gates[:, :, None], 0.0), axis=1)


def plain_layer(devices, rows, routes, gates, gate_up, down):
    dense = lax.all_gather(dense_gates(routes, gates, devices), "inner", axis=0, tiled=True)
    column = lax.dynamic_slice_in_dim(dense, lax.axis_index("inner"), 1, axis=1)
    everyone = lax.all_gather(rows, "inner", axis=0, tiled=True)
    width = down.shape[1]
    projected = jnp.dot(everyone, gate_up[0], preferred_element_type=jnp.float32)
    inner = narrow(jax.nn.silu(projected[:, :width]) * projected[:, width:])
    share = narrow(jnp.dot(inner, down[0], preferred_element_type=jnp.float32) * column)
    total = lax.psum_scatter(share, "inner", scatter_dimension=0, tiled=True)
    return narrow(wide(rows) + wide(total))


def plain_merge(after_first, merged_in, weight):
    columns = lax.all_to_all(merged_in, "inner", split_axis=1, concat_axis=0, tiled=True)
    partial = narrow(jnp.dot(columns, weight, preferred_element_type=jnp.float32))
    merged = lax.psum_scatter(partial, "inner", scatter_dimension=0, tiled=True)
    return narrow(wide(after_first) + jax.nn.silu(wide(merged)))


def unfused(hidden_rows, token_embed, first_routes, first_gates, first_gate_up, first_down,
            second_routes, second_gates, second_gate_up, second_down, hidden_gain, embed_gain,
            merge_weight):
    devices = lax.axis_size("inner")
    after_first = plain_layer(
        devices, hidden_rows, first_routes, first_gates, first_gate_up, first_down
    )
    merged_in = jnp.concatenate(
        [rms_scale(after_first, hidden_gain), rms_scale(token_embed, embed_gain)], axis=1
    )
    after_merge = plain_merge(after_first, merged_in, merge_weight)
    return plain_layer(devices, after_merge, second_routes, second_gates, second_gate_up, second_down)


def local(hidden_rows, *others):
    devices = lax.axis_size("inner")
    tok, width = hidden_rows.shape
    fits = (
        12 * devices * tok * width * 2 <= VMEM_LIMIT
        and devices % 4 == 0 and devices >= 16 and tok % 32 == 0
    )
    return (fused if fits else unfused)(hidden_rows, *others)


def solution(mesh):
    rows = P(("groups", "inner"), None)
    return jax.shard_map(
        local,
        mesh=mesh,
        in_specs=(
            rows, rows, rows, rows,
            P("inner", None, None),
            P("inner", None, None),
            rows, rows,
            P("inner", None, None),
            P("inner", None, None),
            P(),
            P(),
            P("inner", None),
        ),
        out_specs=rows,
        check_vma=False,
    )
```

```python
import functools

import jax
import jax.numpy as jnp
from jax import lax
from jax.experimental import pallas as pl
from jax.experimental.pallas import tpu as pltpu
from jax.sharding import PartitionSpec as P

EPSILON = 1e-06
LANES = 128
CUTS = 4
VMEM_LIMIT = 60 * 1024 * 1024


class Ring:
    def __init__(self, devices, tok):
        self.devices, self.tok = devices, tok
        self.chips = devices // 2
        self.reach = self.chips // 2
        self.rise = self.chips // 2
        me = lax.axis_index("inner")
        chip = me // 2
        across = chip % 2
        along = chip // 2
        self.core = me % 2
        self.place = along * (1 - across) + (2 * self.rise - 1 - along) * across
        self.me = me
        self.spans = [(0, 0)]
        for distance in range(1, self.reach):
            self.spans += [(distance, 0), (distance, 1)]
        self.spans.append((self.reach, 0))

    def device(self, shift, other):
        place = (self.place + shift + self.chips) % self.chips
        across = place // self.rise
        along = place * (1 - across) + (2 * self.rise - 1 - place) * across
        core = self.core * (1 - other) + (1 - self.core) * other
        return (along * 2 + across) * 2 + core

    def first(self, distance, s):
        if distance == 0:
            return ((self.reach - 1) * 4 + 2) * self.tok
        return ((distance - 1) * 4 + 2 * s) * self.tok

    def rows(self, distance, s):
        return pl.ds(self.first(distance, s), 2 * self.tok)

    def side(self, distance, s, other):
        return pl.ds(self.first(distance, s) + other * self.tok, self.tok)

    def half(self, way, distance, other, k):
        part = self.tok // 2
        if distance == 0:
            s, column = 0, k
        elif distance == self.reach:
            s, column = 0, k
        else:
            s, column = (0 if k == way else 1), way
        return pl.ds(self.first(distance, s) + other * self.tok + column * part, part)

    def chunk(self, way, distance, k):
        if distance == self.reach:
            return way
        return 2 + (way * (self.reach - 1) + distance - 1) * 2 + k

    def slot(self, way, distance, other):
        if distance == 0:
            return (self.reach - 1) * 4 + 2 + other
        if distance == self.reach:
            return (self.reach - 1) * 4 + other
        return (distance - 1) * 4 + way * 2 + other


def remote(src, dst, send, recv, device):
    return pltpu.make_async_remote_copy(
        src_ref=src, dst_ref=dst, send_sem=send, recv_sem=recv,
        device_id={"inner": device}, device_id_type=pl.DeviceIdType.MESH,
    )


def wide(values):
    return values.astype(jnp.float32)


def narrow(values):
    return values.astype(jnp.bfloat16)


def sent(ring, whole, sem):
    remote(whole, whole, sem, sem, ring.device(0, 1)).wait_send()


class Reduce:
    def __init__(self, ring, bufs, recvs):
        self.ring = ring
        self.share, self.paired, self.arrived, self.send = bufs
        self.pair_recv, self.recv = recvs
        self.cut = self.share.shape[1] // CUTS

    def pair_copy(self, distance, s):
        ring = self.ring
        slot = ring.spans.index((distance, s))
        here = self.paired.at[pl.ds(slot * ring.tok, ring.tok)]
        return remote(
            self.share.at[ring.side(distance, s, 1)], here,
            self.send.at[0], self.pair_recv.at[slot], ring.device(0, 1),
        ), here

    def start_pair(self, distance, s):
        self.pair_copy(distance, s)[0].start()

    def finish_pair(self, distance, s):
        copy, here = self.pair_copy(distance, s)
        copy.wait_recv()
        rows = self.ring.side(distance, s, 0)
        self.share[rows, :] = narrow(wide(self.share[rows, :]) + wide(here[...]))

    def columns(self, c):
        return pl.ds(c * self.cut, self.cut)

    def hop(self, way, distance, k, c):
        ring = self.ring
        rows = ring.tok // 2
        slot = ring.chunk(way, distance, k)
        landing = self.arrived.at[pl.ds(slot * rows, rows), self.columns(c)]
        return remote(
            self.share.at[ring.half(1 - way, distance, 0, k), self.columns(c)], landing,
            self.send.at[1], self.recv.at[slot * CUTS + c],
            ring.device(1 - 2 * way, 0),
        ), landing

    def launch(self, distance, flip):
        for c in range(CUTS):
            for way in (0, 1):
                self.hop(way, distance, 1 - way if flip else way, c)[0].start()

    def step(self, distance, flip, cuts=range(CUTS)):
        for c in cuts:
            for way in (0, 1):
                k = 1 - way if flip else way
                copy, landing = self.hop(way, distance + 1, k, c)
                copy.wait_recv()
                at = (self.ring.half(1 - way, distance, 0, k), self.columns(c))
                self.share[at] = narrow(wide(self.share[at]) + wide(landing[...]))
                self.hop(way, distance, k, c)[0].start()

    def drain(self):
        ring = self.ring
        sent(ring, self.share.at[pl.ds(0, 2 * ring.reach * ring.tok)], self.send.at[0])
        sent(ring, self.share.at[pl.ds(0, (2 * ring.reach - 1) * ring.tok)], self.send.at[1])

    def piece(self, c):
        halves = []
        for k in (0, 1):
            piece = wide(self.share[self.ring.half(0, 0, 0, k), self.columns(c)])
            for way in (0, 1):
                copy, landing = self.hop(way, 1, k, c)
                copy.wait_recv()
                piece = piece + wide(landing[...])
            halves.append(piece)
        return jnp.concatenate(halves, axis=0)

    def total(self):
        return jnp.concatenate([self.piece(c) for c in range(CUTS)], axis=1)


def reduce_scratch(devices, tok, width):
    reach = devices // 4
    return [
        pltpu.VMEM((devices * tok, width), jnp.bfloat16),
        pltpu.VMEM((2 * reach * tok, width), jnp.bfloat16),
        pltpu.VMEM(((2 * reach - 1) * tok, width), jnp.bfloat16),
        pltpu.SemaphoreType.DMA((2,)),
    ]


def reduce_recvs(devices):
    reach = devices // 4
    return [
        pltpu.SemaphoreType.DMA((2 * reach,)),
        pltpu.SemaphoreType.DMA(((4 * reach - 2) * CUTS,)),
    ]


def gather_scratch(devices, tok, width):
    return [
        pltpu.VMEM((devices * tok, width), jnp.bfloat16),
        pltpu.SemaphoreType.DMA((2,)),
    ]


def normed(values, gain):
    widened = wide(values)
    inverse_rms = lax.rsqrt(jnp.mean(widened * widened, axis=-1, keepdims=True) + EPSILON)
    return narrow(widened * inverse_rms * gain)


def gate_lanes(devices, turned, tables):
    rows = tables[0][0].shape[1]
    turned[...] = jnp.zeros_like(turned)
    for layer, (routes, gates) in enumerate(tables):
        base = 2 * layer * devices
        expert = lax.broadcasted_iota(jnp.int32, (devices, rows), 0)
        dense = jnp.zeros((devices, rows), jnp.float32)
        for k in range(routes.shape[0]):
            dense = dense + jnp.where(expert == routes[k : k + 1, :], gates[k : k + 1, :], 0.0)
        high = wide(narrow(dense))
        turned[base : base + devices, :rows] = high
        turned[base + devices : base + 2 * devices, :rows] = dense - high
    return narrow(turned[...].T[:rows, :])


def block_kernel(devices, *refs):
    (routes1, gates1, routes2, gates2, hidden_gain, embed_gain, hidden_ref, embed_ref,
     gu1_ref, down1_ref, weight_ref, gu2_ref, down2_ref, out_ref) = refs[:14]
    scratch = list(refs[14:])
    take = lambda count: [scratch.pop(0) for _ in range(count)]
    gu1, down1, weight, gu2, down2, load_sem = take(6)
    turned, embed, after_first, pieces, landed, inner = take(6)
    piece_send, piece_recv, own_sem, ring_recv, sib_recv = take(5)
    gather1, gather2 = take(2), take(2)
    reduce1, reduce2, reduce3 = take(4), take(4), take(4)
    recvs1, recvs2 = take(2), take(2)
    tok, width = hidden_ref.shape
    hidden = down1.shape[0]
    depth = weight.shape[0]
    lanes = gather1[0].shape[1] - width
    ring = Ring(devices, tok)
    reach = ring.reach
    part = tok // 2

    barrier = pltpu.get_barrier_semaphore()
    neighbours = [ring.device(1, 0), ring.device(-1, 0), ring.device(0, 1)]
    for device in neighbours:
        pl.semaphore_signal(
            barrier, inc=1, device_id={"inner": device}, device_id_type=pl.DeviceIdType.MESH
        )
    own_rows = ring.side(0, 0, 0)
    loads = [
        pltpu.make_async_copy(source, target, load_sem.at[i])
        for i, (source, target) in enumerate(
            [(hidden_ref, gather1[0].at[own_rows, pl.ds(0, width)]), (embed_ref, embed),
             (gu1_ref.at[0], gu1), (down1_ref.at[0], down1), (weight_ref, weight),
             (gu2_ref.at[0], gu2), (down2_ref.at[0], down2)]
        )
    ]
    waiting = list(range(len(loads)))

    def need(*which):
        for i in which:
            if i in waiting:
                waiting.remove(i)
                loads[i].wait()

    def begin(copy):
        copy.start()

    partners = [(0, 0, 1)]
    for distance in range(1, reach + 1):
        for other in (0, 1):
            partners.append((0, distance, other))
            if distance < reach:
                partners.append((1, distance, other))

    def streams(s):
        return [(way, 1 - way if s else way) for way in (0, 1)]

    def ring_copy(bufs, way, distance, k, cut=None):
        everyone, send = bufs
        slot = ring.chunk(way, distance, k)
        rows = ring.half(way, max(distance - 1, 0), 0, k)
        landing = ring.half(way, distance, 0, k)
        cut = pl.ds(0, everyone.shape[1]) if cut is None else cut
        return remote(
            everyone.at[rows, cut], everyone.at[landing, cut], send.at[0], ring_recv.at[slot],
            ring.device(1 - 2 * way, 0),
        )

    def sibling_copy(bufs, way, distance, k):
        everyone, send = bufs
        if distance == 0:
            s, origin, landing = 0, own_rows, ring.side(0, 0, 1)
        else:
            s = 0 if distance == reach or k == way else 1
            origin, landing = ring.half(way, distance, 0, k), ring.half(way, distance, 1, k)
        return remote(
            everyone.at[origin], everyone.at[landing], send.at[1],
            sib_recv.at[ring.spans.index((distance, s))], ring.device(0, 1),
        )

    def first_sends():
        everyone, send = gather1
        narrow_cut, lane_cut = pl.ds(0, width), pl.ds(width, lanes)

        def send_rows(way, k):
            return remote(
                hidden_ref.at[pl.ds(k * part, part)],
                everyone.at[ring.half(way, 1, 0, k), narrow_cut],
                send.at[0], ring_recv.at[ring.chunk(way, 1, k)], ring.device(1 - 2 * way, 0),
            )

        def send_lanes(way, k):
            return remote(
                everyone.at[ring.half(way, 0, 0, k), lane_cut],
                everyone.at[ring.half(way, 1, 0, k), lane_cut],
                send.at[0], ring_recv.at[ring.chunk(way, 1, k)], ring.device(1 - 2 * way, 0),
            )

        for load in loads:
            load.start()
        everyone[own_rows, lane_cut] = gate_lanes(
            devices, turned, [(routes1[...], gates1[...]), (routes2[...], gates2[...])]
        )
        pl.semaphore_wait(barrier, len(neighbours))
        for way, k in streams(0):
            begin(send_rows(way, k))
            begin(send_lanes(way, k))
        begin(remote(
            hidden_ref, everyone.at[ring.side(0, 0, 1), narrow_cut],
            send.at[1], sib_recv.at[0], ring.device(0, 1),
        ))
        begin(remote(
            everyone.at[own_rows, lane_cut], everyone.at[ring.side(0, 0, 1), lane_cut],
            send.at[1], sib_recv.at[0], ring.device(0, 1),
        ))
        for way, k in streams(1):
            begin(send_rows(way, k))
            begin(send_lanes(way, k))

    def layer(bufs, first, reducing, load_ids, gu, down, meanwhile):
        everyone = bufs[0]
        share = reducing.share
        gate_rows = gather1[0]
        step = min(256, hidden)
        steps = hidden // step

        def pass_on(distance, s):
            for way, k in streams(s):
                ring_copy(bufs, way, distance, k).wait_recv()
                if distance + 1 < reach or (distance + 1 == reach and s == 0):
                    begin(ring_copy(bufs, way, distance + 1, k))
                begin(sibling_copy(bufs, way, distance, k))

        def from_sibling(distance, s):
            both = bufs[0].at[ring.side(distance, s, 1)]
            remote(
                both, both, bufs[1].at[1], sib_recv.at[ring.spans.index((distance, s))],
                ring.device(0, 1),
            ).wait_recv()

        def up(first_row, count, low, high):
            rows = pl.ds(first_row, count)

            for j in range(low, high):
                left, right = pl.ds(j * step, step), pl.ds(hidden + j * step, step)
                x = everyone[rows, :width]
                g = jnp.dot(x, gu[:, left], preferred_element_type=jnp.float32)
                u = jnp.dot(x, gu[:, right], preferred_element_type=jnp.float32)
                inner[:count, left] = narrow(jax.nn.silu(g) * u)

        def finish(first_row, count, *spans):
            rows = pl.ds(first_row, count)
            lane = lax.broadcasted_iota(jnp.int32, (count, lanes), 1)
            mine = (lane == ring.me + first * devices) | (lane == ring.me + (first + 1) * devices)
            gate = jnp.sum(
                jnp.where(mine, wide(gate_rows[rows, width:]), 0.0), axis=1, keepdims=True
            )
            span = min(512, width)

            for j in range(width // span):
                cut = pl.ds(j * span, span)
                out = jnp.dot(
                    inner[:count, :], down[:, cut], preferred_element_type=jnp.float32
                )
                share[rows, cut] = narrow(out * gate)

            for at in spans:
                reducing.start_pair(*at)

        last = reach - 1
        spans = ring.spans
        from_sibling(0, 0)
        need(load_ids[0])
        up(ring.first(0, 0), 2 * tok, 0, steps)
        pass_on(1, 0)
        need(load_ids[1])
        finish(ring.first(0, 0), 2 * tok, (0, 0))
        meanwhile()
        for at, span in enumerate(spans[1:-1], 1):
            from_sibling(*span)
            up(ring.first(*span), 2 * tok, 0, steps // 2)
            if span == (last, 1):
                reducing.finish_pair(last, 0)
                reducing.launch(last, True)
            up(ring.first(*span), 2 * tok, steps // 2, steps)
            pass_on(*spans[at + 1])
            finish(ring.first(*span), 2 * tok, span)
            if span != (last, 1):
                reducing.finish_pair(*spans[at - 1])
        from_sibling(reach, 0)
        up(ring.first(reach, 0), 2 * tok, 0, steps // 2)
        reducing.step(last - 1, True, range(0, 1))
        up(ring.first(reach, 0), 2 * tok, steps // 2, steps)
        reducing.step(last - 1, True, range(1, CUTS - 1))
        finish(ring.first(reach, 0), 2 * tok, (reach, 0))
        reducing.step(last - 1, True, range(CUTS - 1, CUTS))
        reducing.finish_pair(reach, 0)
        reducing.launch(reach, False)
        reducing.finish_pair(last, 1)
        for distance in range(last, 0, -1):
            if distance > 2:
                reducing.step(distance - 2, True)
            reducing.step(distance, False)

    def target_of(way, distance, other):
        return ring.device(distance * (1 - 2 * way), other)

    def piece(way, distance, other):
        target = target_of(way, distance, other)
        slot = ring.slot(way, distance, other)
        return remote(
            pieces.at[target], landed.at[pl.ds(slot * tok, tok)],
            piece_send.at[0], piece_recv.at[distance], target,
        )

    def send_pieces():
        for partner in reversed(partners):
            begin(piece(*partner))

    def merge(reducing):
        own = pltpu.make_async_copy(
            pieces.at[ring.me], landed.at[pl.ds(ring.slot(0, 0, 0) * tok, tok)], own_sem.at[0]
        )
        own.start()
        need(4)
        share = reducing.share
        came = set()

        def arrive(distance):
            if distance not in came:
                came.add(distance)
                low = min(ring.slot(*p) for p in partners if p[1] == distance)
                count = sum(p[1] == distance for p in partners)
                whole = landed.at[pl.ds(low * tok, count * tok)]
                remote(
                    whole, whole, piece_send.at[0], piece_recv.at[distance], ring.device(0, 1)
                ).wait_recv()
                if distance == 0:
                    own.wait()

        def product(distance, s):
            arrive(distance)
            pick = []
            for other in (0, 1):
                for column in (0, 1):
                    if distance in (0, reach):
                        way, k = 0, column
                    else:
                        way, k = column, (column if s == 0 else 1 - column)
                    row = ring.slot(way, distance, other) * tok + k * part
                    pick.append(landed[row : row + part, :])
            x = jnp.concatenate(pick, axis=0)
            rows = ring.rows(distance, s)
            span = min(512, width)
            for j in range(width // span):
                cut = pl.ds(j * span, span)
                share[rows, cut] = narrow(
                    jnp.dot(x, weight[:, cut], preferred_element_type=jnp.float32)
                )
            reducing.start_pair(distance, s)

        last = reach - 1
        product(reach, 0)
        product(last, 0)
        reducing.finish_pair(reach, 0)
        reducing.launch(reach, False)
        product(last, 1)
        reducing.finish_pair(last, 0)
        reducing.launch(last, True)
        product(last - 1, 0)
        reducing.finish_pair(last, 1)
        for distance in range(last, 0, -1):
            if distance > 1:
                product(distance - 1, 1)
                reducing.finish_pair(distance - 1, 0)
            else:
                product(0, 0)
            reducing.step(distance, False)
            if distance > 1:
                if distance > 2:
                    product(distance - 2, 0)
                reducing.finish_pair(distance - 1, 1)
                reducing.step(distance - 1, True)
        reducing.finish_pair(0, 0)

    def scatter_pieces(values, at):
        for j in range(width // depth):
            pieces[at + j] = values[:, j * depth : (j + 1) * depth]

    def embed_pieces():
        need(1)
        scatter_pieces(normed(embed[...], embed_gain[...]), width // depth)

    first_sends()
    need(0)
    reducing1 = reducing = Reduce(ring, reduce1, recvs1)
    layer(gather1, 0, reducing, (2, 3), gu1, down1, embed_pieces)
    first = narrow(wide(gather1[0][own_rows, :width]) + reducing.total())
    after_first[...] = first
    scatter_pieces(normed(first, hidden_gain[...]), 0)
    send_pieces()
    reducing2 = reducing = Reduce(ring, reduce2, recvs2)
    merge(reducing)
    everyone, send = gather2
    for c in range(CUTS):
        cut = reducing.columns(c)
        everyone[own_rows, cut] = narrow(
            wide(after_first[:, cut]) + jax.nn.silu(reducing.piece(c))
        )
        for way, k in streams(0):
            begin(ring_copy(gather2, way, 1, k, cut))
    for way, k in streams(1):
        begin(ring_copy(gather2, way, 1, k))
    begin(sibling_copy(gather2, 0, 0, 0))
    reducing3 = reducing = Reduce(ring, reduce3, recvs2)
    layer(gather2, 2, reducing, (5, 6), gu2, down2, lambda: None)
    out_ref[...] = narrow(wide(gather2[0][own_rows, :]) + reducing.total())
    for everyone, send in (gather1, gather2):
        sent(ring, everyone.at[pl.ds(0, (2 * reach - 1) * tok)], send.at[0])
        sent(ring, everyone.at[pl.ds(0, 2 * reach * tok)], send.at[1])
    sent(ring, landed.at[pl.ds(0, (devices - 1) * tok)], piece_send.at[0])
    for each in (reducing1, reducing2, reducing3):
        each.drain()


def fused(hidden_rows, token_embed, first_routes, first_gates, first_gate_up, first_down,
          second_routes, second_gates, second_gate_up, second_down, hidden_gain, embed_gain,
          merge_weight):
    devices = lax.axis_size("inner")
    tok, width = hidden_rows.shape
    hidden = first_down.shape[1]
    depth = merge_weight.shape[0]
    lanes = -(-4 * devices // LANES) * LANES
    reach = devices // 4
    vmem = pl.BlockSpec(memory_space=pltpu.VMEM)
    hbm = pl.BlockSpec(memory_space=pl.ANY)
    bf16 = jnp.bfloat16
    scratch = [
        pltpu.VMEM(first_gate_up.shape[1:], bf16),
        pltpu.VMEM(first_down.shape[1:], bf16),
        pltpu.VMEM(merge_weight.shape, bf16),
        pltpu.VMEM(second_gate_up.shape[1:], bf16),
        pltpu.VMEM(second_down.shape[1:], bf16),
        pltpu.SemaphoreType.DMA((7,)),
        pltpu.VMEM((lanes, -(-tok // LANES) * LANES), jnp.float32),
        pltpu.VMEM((tok, width), bf16),
        pltpu.VMEM((tok, width), bf16),
        pltpu.VMEM((devices, tok, depth), bf16),
        pltpu.VMEM((devices * tok, depth), bf16),
        pltpu.VMEM((4 * tok, hidden), bf16),
        pltpu.SemaphoreType.DMA((1,)),
        pltpu.SemaphoreType.DMA((reach + 1,)),
        pltpu.SemaphoreType.DMA((1,)),
        pltpu.SemaphoreType.DMA((4 * reach - 2,)),
        pltpu.SemaphoreType.DMA((2 * reach,)),
    ]
    scratch += gather_scratch(devices, tok, width + lanes) + gather_scratch(devices, tok, width)
    for _ in range(3):
        scratch += reduce_scratch(devices, tok, width)
    scratch += reduce_recvs(devices) + reduce_recvs(devices)
    return pl.pallas_call(
        functools.partial(block_kernel, devices),
        out_shape=jax.ShapeDtypeStruct((tok, width), bf16),
        in_specs=[vmem] * 6 + [hbm] * 7,
        out_specs=vmem,
        scratch_shapes=scratch,
        compiler_params=pltpu.CompilerParams(
            collective_id=0, has_side_effects=True, vmem_limit_bytes=VMEM_LIMIT
        ),
    )(first_routes.T, first_gates.T, second_routes.T, second_gates.T, hidden_gain[None],
      embed_gain[None], hidden_rows, token_embed, first_gate_up, first_down, merge_weight,
      second_gate_up, second_down)


def rms_scale(values, gain_vec):
    widened = values.astype(jnp.float32)
    inverse_rms = lax.rsqrt(jnp.mean(widened * widened, axis=-1, keepdims=True) + EPSILON)
    return (widened * inverse_rms * gain_vec).astype(jnp.bfloat16)


def dense_gates(routes, gates, experts):
    hit = routes[:, :, None] == jnp.arange(experts, dtype=jnp.int32)[None, None, :]
    return jnp.sum(jnp.where(hit, gates[:, :, None], 0.0), axis=1)


def plain_layer(devices, rows, routes, gates, gate_up, down):
    dense = lax.all_gather(dense_gates(routes, gates, devices), "inner", axis=0, tiled=True)
    column = lax.dynamic_slice_in_dim(dense, lax.axis_index("inner"), 1, axis=1)
    everyone = lax.all_gather(rows, "inner", axis=0, tiled=True)
    width = down.shape[1]
    projected = jnp.dot(everyone, gate_up[0], preferred_element_type=jnp.float32)
    inner = narrow(jax.nn.silu(projected[:, :width]) * projected[:, width:])
    share = narrow(jnp.dot(inner, down[0], preferred_element_type=jnp.float32) * column)
    total = lax.psum_scatter(share, "inner", scatter_dimension=0, tiled=True)
    return narrow(wide(rows) + wide(total))


def plain_merge(after_first, merged_in, weight):
    columns = lax.all_to_all(merged_in, "inner", split_axis=1, concat_axis=0, tiled=True)
    partial = narrow(jnp.dot(columns, weight, preferred_element_type=jnp.float32))
    merged = lax.psum_scatter(partial, "inner", scatter_dimension=0, tiled=True)
    return narrow(wide(after_first) + jax.nn.silu(wide(merged)))


def unfused(hidden_rows, token_embed, first_routes, first_gates, first_gate_up, first_down,
            second_routes, second_gates, second_gate_up, second_down, hidden_gain, embed_gain,
            merge_weight):
    devices = lax.axis_size("inner")
    after_first = plain_layer(
        devices, hidden_rows, first_routes, first_gates, first_gate_up, first_down
    )
    merged_in = jnp.concatenate(
        [rms_scale(after_first, hidden_gain), rms_scale(token_embed, embed_gain)], axis=1
    )
    after_merge = plain_merge(after_first, merged_in, merge_weight)
    return plain_layer(devices, after_merge, second_routes, second_gates, second_gate_up, second_down)


def local(hidden_rows, *others):
    devices = lax.axis_size("inner")
    tok, width = hidden_rows.shape
    fits = (
        12 * devices * tok * width * 2 <= VMEM_LIMIT
        and devices % 4 == 0 and devices >= 16 and tok % 32 == 0
    )
    return (fused if fits else unfused)(hidden_rows, *others)


def solution(mesh):
    rows = P(("groups", "inner"), None)
    return jax.shard_map(
        local,
        mesh=mesh,
        in_specs=(
            rows, rows, rows, rows,
            P("inner", None, None),
            P("inner", None, None),
            rows, rows,
            P("inner", None, None),
            P("inner", None, None),
            P(),
            P(),
            P("inner", None),
        ),
        out_specs=rows,
        check_vma=False,
    )
```

```python
import functools

import jax
import jax.numpy as jnp
from jax import lax
from jax.experimental import pallas as pl
from jax.experimental.pallas import tpu as pltpu
from jax.sharding import PartitionSpec as P

EPSILON = 1e-06
LANES = 128
CUTS = 4
VMEM_LIMIT = 60 * 1024 * 1024


class Ring:
    def __init__(self, devices, tok):
        self.devices, self.tok = devices, tok
        self.chips = devices // 2
        self.reach = self.chips // 2
        self.rise = self.chips // 2
        me = lax.axis_index("inner")
        chip = me // 2
        across = chip % 2
        along = chip // 2
        self.core = me % 2
        self.place = along * (1 - across) + (2 * self.rise - 1 - along) * across
        self.me = me
        self.spans = [(0, 0)]
        for distance in range(1, self.reach):
            self.spans += [(distance, 0), (distance, 1)]
        self.spans.append((self.reach, 0))

    def device(self, shift, other):
        place = (self.place + shift + self.chips) % self.chips
        across = place // self.rise
        along = place * (1 - across) + (2 * self.rise - 1 - place) * across
        core = self.core * (1 - other) + (1 - self.core) * other
        return (along * 2 + across) * 2 + core

    def first(self, distance, s):
        if distance == 0:
            return ((self.reach - 1) * 4 + 2) * self.tok
        return ((distance - 1) * 4 + 2 * s) * self.tok

    def rows(self, distance, s):
        return pl.ds(self.first(distance, s), 2 * self.tok)

    def side(self, distance, s, other):
        return pl.ds(self.first(distance, s) + other * self.tok, self.tok)

    def half(self, way, distance, other, k):
        part = self.tok // 2
        if distance == 0:
            s, column = 0, k
        elif distance == self.reach:
            s, column = 0, k
        else:
            s, column = (0 if k == way else 1), way
        return pl.ds(self.first(distance, s) + other * self.tok + column * part, part)

    def chunk(self, way, distance, k):
        if distance == self.reach:
            return way
        return 2 + (way * (self.reach - 1) + distance - 1) * 2 + k

    def slot(self, way, distance, other):
        if distance == 0:
            return (self.reach - 1) * 4 + 2 + other
        if distance == self.reach:
            return (self.reach - 1) * 4 + other
        return (distance - 1) * 4 + way * 2 + other


def remote(src, dst, send, recv, device):
    return pltpu.make_async_remote_copy(
        src_ref=src, dst_ref=dst, send_sem=send, recv_sem=recv,
        device_id={"inner": device}, device_id_type=pl.DeviceIdType.MESH,
    )


def wide(values):
    return values.astype(jnp.float32)


def narrow(values):
    return values.astype(jnp.bfloat16)


def sent(ring, whole, sem):
    remote(whole, whole, sem, sem, ring.device(0, 1)).wait_send()


class Reduce:
    def __init__(self, ring, bufs, recvs):
        self.ring = ring
        self.share, self.paired, self.arrived, self.send = bufs
        self.pair_recv, self.recv = recvs
        self.cut = self.share.shape[1] // CUTS

    def pair_copy(self, distance, s):
        ring = self.ring
        slot = ring.spans.index((distance, s))
        here = self.paired.at[pl.ds(slot * ring.tok, ring.tok)]
        return remote(
            self.share.at[ring.side(distance, s, 1)], here,
            self.send.at[0], self.pair_recv.at[slot], ring.device(0, 1),
        ), here

    def start_pair(self, distance, s):
        self.pair_copy(distance, s)[0].start()

    def finish_pair(self, distance, s):
        copy, here = self.pair_copy(distance, s)
        copy.wait_recv()
        rows = self.ring.side(distance, s, 0)
        self.share[rows, :] = narrow(wide(self.share[rows, :]) + wide(here[...]))

    def columns(self, c):
        return pl.ds(c * self.cut, self.cut)

    def far_copy(self, c):
        ring = self.ring
        slot = 2 * ring.reach - 1
        here = self.paired.at[pl.ds(slot * ring.tok, ring.tok), self.columns(c)]
        return remote(
            self.share.at[ring.side(ring.reach, 0, 1), self.columns(c)], here,
            self.send.at[0], self.pair_recv.at[slot + c], ring.device(0, 1),
        ), here

    def launch_far(self):
        ring = self.ring
        for c in range(CUTS):
            copy, here = self.far_copy(c)
            copy.wait_recv()
            at = (ring.side(ring.reach, 0, 0), self.columns(c))
            self.share[at] = narrow(wide(self.share[at]) + wide(here[...]))
            for way in (0, 1):
                self.hop(way, ring.reach, way, c)[0].start()

    def hop(self, way, distance, k, c):
        ring = self.ring
        rows = ring.tok // 2
        slot = ring.chunk(way, distance, k)
        landing = self.arrived.at[pl.ds(slot * rows, rows), self.columns(c)]
        return remote(
            self.share.at[ring.half(1 - way, distance, 0, k), self.columns(c)], landing,
            self.send.at[1], self.recv.at[slot * CUTS + c],
            ring.device(1 - 2 * way, 0),
        ), landing

    def launch(self, distance, flip):
        for c in range(CUTS):
            for way in (0, 1):
                self.hop(way, distance, 1 - way if flip else way, c)[0].start()

    def step(self, distance, flip, cuts=range(CUTS)):
        for c in cuts:
            for way in (0, 1):
                k = 1 - way if flip else way
                copy, landing = self.hop(way, distance + 1, k, c)
                copy.wait_recv()
                at = (self.ring.half(1 - way, distance, 0, k), self.columns(c))
                self.share[at] = narrow(wide(self.share[at]) + wide(landing[...]))
                self.hop(way, distance, k, c)[0].start()

    def drain(self):
        ring = self.ring
        sent(ring, self.share.at[pl.ds(0, 2 * ring.reach * ring.tok)], self.send.at[0])
        sent(ring, self.share.at[pl.ds(0, (2 * ring.reach - 1) * ring.tok)], self.send.at[1])

    def piece(self, c):
        halves = []
        for k in (0, 1):
            piece = wide(self.share[self.ring.half(0, 0, 0, k), self.columns(c)])
            for way in (0, 1):
                copy, landing = self.hop(way, 1, k, c)
                copy.wait_recv()
                piece = piece + wide(landing[...])
            halves.append(piece)
        return jnp.concatenate(halves, axis=0)

    def total(self):
        return jnp.concatenate([self.piece(c) for c in range(CUTS)], axis=1)


def reduce_scratch(devices, tok, width):
    reach = devices // 4
    return [
        pltpu.VMEM((devices * tok, width), jnp.bfloat16),
        pltpu.VMEM((2 * reach * tok, width), jnp.bfloat16),
        pltpu.VMEM(((2 * reach - 1) * tok, width), jnp.bfloat16),
        pltpu.SemaphoreType.DMA((2,)),
    ]


def reduce_recvs(devices):
    reach = devices // 4
    return [
        pltpu.SemaphoreType.DMA((2 * reach - 1 + CUTS,)),
        pltpu.SemaphoreType.DMA(((4 * reach - 2) * CUTS,)),
    ]


def gather_scratch(devices, tok, width):
    return [
        pltpu.VMEM((devices * tok, width), jnp.bfloat16),
        pltpu.SemaphoreType.DMA((2,)),
    ]


def normed(values, gain):
    widened = wide(values)
    inverse_rms = lax.rsqrt(jnp.mean(widened * widened, axis=-1, keepdims=True) + EPSILON)
    return narrow(widened * inverse_rms * gain)


def gate_lanes(devices, turned, tables):
    rows = tables[0][0].shape[1]
    turned[...] = jnp.zeros_like(turned)
    for layer, (routes, gates) in enumerate(tables):
        base = 2 * layer * devices
        expert = lax.broadcasted_iota(jnp.int32, (devices, rows), 0)
        dense = jnp.zeros((devices, rows), jnp.float32)
        for k in range(routes.shape[0]):
            dense = dense + jnp.where(expert == routes[k : k + 1, :], gates[k : k + 1, :], 0.0)
        high = wide(narrow(dense))
        turned[base : base + devices, :rows] = high
        turned[base + devices : base + 2 * devices, :rows] = dense - high
    return narrow(turned[...].T[:rows, :])


def block_kernel(devices, *refs):
    smalls = refs[:6]
    hidden_ref, embed_ref, gu1_ref, down1_ref, weight_ref, gu2_ref, down2_ref, out_ref = refs[6:14]
    scratch = list(refs[14:])
    take = lambda count: [scratch.pop(0) for _ in range(count)]
    gu1, down1, weight, gu2, down2, load_sem = take(6)
    turned, embed, after_first, pieces, landed, inner = take(6)
    piece_send, piece_recv, own_sem, ring_recv, sib_recv = take(5)
    gather1, gather2 = take(2), take(2)
    reduce1, reduce2, reduce3 = take(4), take(4), take(4)
    recvs1, recvs2 = take(2), take(2)
    out, out_sem = take(2)
    routes1, gates1, routes2, gates2, hidden_gain, embed_gain = held = take(6)
    tok, width = hidden_ref.shape
    hidden = down1.shape[0]
    depth = weight.shape[0]
    lanes = gather1[0].shape[1] - width
    ring = Ring(devices, tok)
    reach = ring.reach
    part = tok // 2

    barrier = pltpu.get_barrier_semaphore()
    neighbours = [ring.device(1, 0), ring.device(-1, 0), ring.device(0, 1)]
    for device in neighbours:
        pl.semaphore_signal(
            barrier, inc=1, device_id={"inner": device}, device_id_type=pl.DeviceIdType.MESH
        )
    own_rows = ring.side(0, 0, 0)
    loads = [
        pltpu.make_async_copy(source, target, load_sem.at[i])
        for i, (source, target) in enumerate(
            [(hidden_ref, gather1[0].at[own_rows, pl.ds(0, width)]), (embed_ref, embed),
             (gu1_ref.at[0], gu1), (down1_ref.at[0], down1), (weight_ref, weight),
             (gu2_ref.at[0], gu2), (down2_ref.at[0], down2), *zip(smalls, held)]
        )
    ]
    for load in loads[7:] + loads[:7]:
        load.start()
    waiting = list(range(len(loads)))

    def need(*which):
        for i in which:
            if i in waiting:
                waiting.remove(i)
                loads[i].wait()

    def begin(copy):
        copy.start()

    partners = [(0, 0, 1)]
    for distance in range(1, reach + 1):
        for other in (0, 1):
            partners.append((0, distance, other))
            if distance < reach:
                partners.append((1, distance, other))

    def streams(s):
        return [(way, 1 - way if s else way) for way in (0, 1)]

    def ring_copy(bufs, way, distance, k, cut=None):
        everyone, send = bufs
        slot = ring.chunk(way, distance, k)
        rows = ring.half(way, max(distance - 1, 0), 0, k)
        landing = ring.half(way, distance, 0, k)
        cut = pl.ds(0, everyone.shape[1]) if cut is None else cut
        return remote(
            everyone.at[rows, cut], everyone.at[landing, cut], send.at[0], ring_recv.at[slot],
            ring.device(1 - 2 * way, 0),
        )

    def sibling_copy(bufs, way, distance, k):
        everyone, send = bufs
        if distance == 0:
            s, origin, landing = 0, own_rows, ring.side(0, 0, 1)
        else:
            s = 0 if distance == reach or k == way else 1
            origin, landing = ring.half(way, distance, 0, k), ring.half(way, distance, 1, k)
        return remote(
            everyone.at[origin], everyone.at[landing], send.at[1],
            sib_recv.at[ring.spans.index((distance, s))], ring.device(0, 1),
        )

    def first_sends():
        everyone, send = gather1
        narrow_cut, lane_cut = pl.ds(0, width), pl.ds(width, lanes)

        def send_rows(way, k):
            return remote(
                hidden_ref.at[pl.ds(k * part, part)],
                everyone.at[ring.half(way, 1, 0, k), narrow_cut],
                send.at[0], ring_recv.at[ring.chunk(way, 1, k)], ring.device(1 - 2 * way, 0),
            )

        def send_lanes(way, k):
            return remote(
                everyone.at[ring.half(way, 0, 0, k), lane_cut],
                everyone.at[ring.half(way, 1, 0, k), lane_cut],
                send.at[0], ring_recv.at[ring.chunk(way, 1, k)], ring.device(1 - 2 * way, 0),
            )

        need(*range(7, len(loads)))
        everyone[own_rows, lane_cut] = gate_lanes(
            devices, turned, [(routes1[...], gates1[...]), (routes2[...], gates2[...])]
        )
        pl.semaphore_wait(barrier, len(neighbours))
        for way, k in streams(0):
            begin(send_rows(way, k))
            begin(send_lanes(way, k))
        begin(remote(
            hidden_ref, everyone.at[ring.side(0, 0, 1), narrow_cut],
            send.at[1], sib_recv.at[0], ring.device(0, 1),
        ))
        begin(remote(
            everyone.at[own_rows, lane_cut], everyone.at[ring.side(0, 0, 1), lane_cut],
            send.at[1], sib_recv.at[0], ring.device(0, 1),
        ))
        for way, k in streams(1):
            begin(send_rows(way, k))
            begin(send_lanes(way, k))

    def layer(bufs, first, reducing, load_ids, gu, down, meanwhile):
        everyone = bufs[0]
        share = reducing.share
        gate_rows = gather1[0]
        step = min(256, hidden)
        steps = hidden // step

        def pass_on(distance, s):
            for way, k in streams(s):
                ring_copy(bufs, way, distance, k).wait_recv()
                if distance + 1 < reach or (distance + 1 == reach and s == 0):
                    begin(ring_copy(bufs, way, distance + 1, k))
                begin(sibling_copy(bufs, way, distance, k))

        def from_sibling(distance, s):
            both = bufs[0].at[ring.side(distance, s, 1)]
            remote(
                both, both, bufs[1].at[1], sib_recv.at[ring.spans.index((distance, s))],
                ring.device(0, 1),
            ).wait_recv()

        def up(first_row, count, low, high):
            rows = pl.ds(first_row, count)

            for j in range(low, high):
                left, right = pl.ds(j * step, step), pl.ds(hidden + j * step, step)
                x = everyone[rows, :width]
                g = jnp.dot(x, gu[:, left], preferred_element_type=jnp.float32)
                u = jnp.dot(x, gu[:, right], preferred_element_type=jnp.float32)
                inner[:count, left] = narrow(jax.nn.silu(g) * u)

        def finish(span):
            count = 2 * tok
            rows = ring.rows(*span)
            lane = lax.broadcasted_iota(jnp.int32, (count, lanes), 1)
            mine = (lane == ring.me + first * devices) | (lane == ring.me + (first + 1) * devices)
            gate = jnp.sum(
                jnp.where(mine, wide(gate_rows[rows, width:]), 0.0), axis=1, keepdims=True
            )
            for c in range(CUTS):
                cut = reducing.columns(c)
                out = jnp.dot(
                    inner[:count, :], down[:, cut], preferred_element_type=jnp.float32
                )
                share[rows, cut] = narrow(out * gate)
                if span == (reach, 0):
                    reducing.far_copy(c)[0].start()

            if span != (reach, 0):
                reducing.start_pair(*span)

        last = reach - 1
        spans = ring.spans
        from_sibling(0, 0)
        need(load_ids[0])
        up(ring.first(0, 0), 2 * tok, 0, steps)
        pass_on(1, 0)
        need(load_ids[1])
        finish((0, 0))
        meanwhile()
        for at, span in enumerate(spans[1:-1], 1):
            if span == (last, 1):
                reducing.finish_pair(last, 0)
                reducing.launch(last, True)
            from_sibling(*span)
            up(ring.first(*span), 2 * tok, 0, steps)
            pass_on(*spans[at + 1])
            finish(span)
            if span != (last, 1):
                reducing.finish_pair(*spans[at - 1])
        from_sibling(reach, 0)
        up(ring.first(reach, 0), 2 * tok, 0, steps // 2)
        reducing.step(last - 1, True, range(0, 1))
        up(ring.first(reach, 0), 2 * tok, steps // 2, steps)
        reducing.step(last - 1, True, range(1, CUTS - 1))
        finish((reach, 0))
        reducing.step(last - 1, True, range(CUTS - 1, CUTS))
        reducing.launch_far()
        reducing.finish_pair(last, 1)
        for distance in range(last, 0, -1):
            if distance > 2:
                reducing.step(distance - 2, True)
            reducing.step(distance, False)

    def target_of(way, distance, other):
        return ring.device(distance * (1 - 2 * way), other)

    def piece(way, distance, other):
        target = target_of(way, distance, other)
        slot = ring.slot(way, distance, other)
        return remote(
            pieces.at[target], landed.at[pl.ds(slot * tok, tok)],
            piece_send.at[0], piece_recv.at[distance], target,
        )

    def send_pieces():
        for partner in reversed(partners):
            begin(piece(*partner))

    def merge(reducing):
        own = pltpu.make_async_copy(
            pieces.at[ring.me], landed.at[pl.ds(ring.slot(0, 0, 0) * tok, tok)], own_sem.at[0]
        )
        own.start()
        need(4)
        share = reducing.share
        came = set()

        def arrive(distance):
            if distance not in came:
                came.add(distance)
                low = min(ring.slot(*p) for p in partners if p[1] == distance)
                count = sum(p[1] == distance for p in partners)
                whole = landed.at[pl.ds(low * tok, count * tok)]
                remote(
                    whole, whole, piece_send.at[0], piece_recv.at[distance], ring.device(0, 1)
                ).wait_recv()
                if distance == 0:
                    own.wait()

        def product(distance, s):
            arrive(distance)
            pick = []
            for other in (0, 1):
                for column in (0, 1):
                    if distance in (0, reach):
                        way, k = 0, column
                    else:
                        way, k = column, (column if s == 0 else 1 - column)
                    row = ring.slot(way, distance, other) * tok + k * part
                    pick.append(landed[row : row + part, :])
            x = jnp.concatenate(pick, axis=0)
            rows = ring.rows(distance, s)
            for c in range(CUTS):
                cut = reducing.columns(c)
                share[rows, cut] = narrow(
                    jnp.dot(x, weight[:, cut], preferred_element_type=jnp.float32)
                )
                if distance == reach:
                    reducing.far_copy(c)[0].start()
            if distance != reach:
                reducing.start_pair(distance, s)

        last = reach - 1
        product(reach, 0)
        product(last, 0)
        reducing.launch_far()
        product(last, 1)
        reducing.finish_pair(last, 0)
        reducing.launch(last, True)
        product(last - 1, 0)
        reducing.finish_pair(last, 1)
        for distance in range(last, 0, -1):
            if distance > 1:
                product(distance - 1, 1)
                reducing.finish_pair(distance - 1, 0)
            else:
                product(0, 0)
            reducing.step(distance, False)
            if distance > 1:
                if distance > 2:
                    product(distance - 2, 0)
                reducing.finish_pair(distance - 1, 1)
                reducing.step(distance - 1, True)
        reducing.finish_pair(0, 0)

    def scatter_pieces(values, at):
        for j in range(width // depth):
            pieces[at + j] = values[:, j * depth : (j + 1) * depth]

    def embed_pieces():
        need(1)
        scatter_pieces(normed(embed[...], embed_gain[...]), width // depth)

    first_sends()
    need(0)
    reducing1 = reducing = Reduce(ring, reduce1, recvs1)
    layer(gather1, 0, reducing, (2, 3), gu1, down1, embed_pieces)
    squares = jnp.zeros((tok, 1), jnp.float32)
    for c in range(CUTS):
        cut = reducing.columns(c)
        first = narrow(wide(gather1[0][own_rows, cut]) + reducing.piece(c))
        after_first[:, cut] = first
        squares = squares + jnp.sum(wide(first) * wide(first), axis=-1, keepdims=True)
    inverse_rms = lax.rsqrt(squares / width + EPSILON)
    for j in range(width // depth):
        cut = pl.ds(j * depth, depth)
        pieces[j] = narrow(wide(after_first[:, cut]) * inverse_rms * hidden_gain[:, cut])
    send_pieces()
    reducing2 = reducing = Reduce(ring, reduce2, recvs2)
    merge(reducing)
    everyone, send = gather2
    for c in range(CUTS):
        cut = reducing.columns(c)
        everyone[own_rows, cut] = narrow(
            wide(after_first[:, cut]) + jax.nn.silu(reducing.piece(c))
        )
        for way, k in streams(0):
            begin(ring_copy(gather2, way, 1, k, cut))
    for way, k in streams(1):
        begin(ring_copy(gather2, way, 1, k))
    begin(sibling_copy(gather2, 0, 0, 0))
    reducing3 = reducing = Reduce(ring, reduce3, recvs2)
    layer(gather2, 2, reducing, (5, 6), gu2, down2, lambda: None)
    stores = []
    for c in range(CUTS):
        cut = reducing.columns(c)
        out[:, cut] = narrow(wide(gather2[0][own_rows, cut]) + reducing.piece(c))
        stores.append(pltpu.make_async_copy(out.at[:, cut], out_ref.at[:, cut], out_sem.at[c]))
        stores[-1].start()
    for everyone, send in (gather1, gather2):
        sent(ring, everyone.at[pl.ds(0, (2 * reach - 1) * tok)], send.at[0])
        sent(ring, everyone.at[pl.ds(0, 2 * reach * tok)], send.at[1])
    sent(ring, landed.at[pl.ds(0, (devices - 1) * tok)], piece_send.at[0])
    for each in (reducing1, reducing2, reducing3):
        each.drain()
    for store in stores:
        store.wait()


def fused(hidden_rows, token_embed, first_routes, first_gates, first_gate_up, first_down,
          second_routes, second_gates, second_gate_up, second_down, hidden_gain, embed_gain,
          merge_weight):
    devices = lax.axis_size("inner")
    tok, width = hidden_rows.shape
    hidden = first_down.shape[1]
    depth = merge_weight.shape[0]
    lanes = -(-4 * devices // LANES) * LANES
    reach = devices // 4
    hbm = pl.BlockSpec(memory_space=pl.ANY)
    bf16 = jnp.bfloat16
    scratch = [
        pltpu.VMEM(first_gate_up.shape[1:], bf16),
        pltpu.VMEM(first_down.shape[1:], bf16),
        pltpu.VMEM(merge_weight.shape, bf16),
        pltpu.VMEM(second_gate_up.shape[1:], bf16),
        pltpu.VMEM(second_down.shape[1:], bf16),
        pltpu.SemaphoreType.DMA((13,)),
        pltpu.VMEM((lanes, -(-tok // LANES) * LANES), jnp.float32),
        pltpu.VMEM((tok, width), bf16),
        pltpu.VMEM((tok, width), bf16),
        pltpu.VMEM((devices, tok, depth), bf16),
        pltpu.VMEM((devices * tok, depth), bf16),
        pltpu.VMEM((4 * tok, hidden), bf16),
        pltpu.SemaphoreType.DMA((1,)),
        pltpu.SemaphoreType.DMA((reach + 1,)),
        pltpu.SemaphoreType.DMA((1,)),
        pltpu.SemaphoreType.DMA((4 * reach - 2,)),
        pltpu.SemaphoreType.DMA((2 * reach,)),
    ]
    scratch += gather_scratch(devices, tok, width + lanes) + gather_scratch(devices, tok, width)
    for _ in range(3):
        scratch += reduce_scratch(devices, tok, width)
    scratch += reduce_recvs(devices) + reduce_recvs(devices)
    scratch += [pltpu.VMEM((tok, width), bf16), pltpu.SemaphoreType.DMA((CUTS,))]
    smalls = (first_routes.T, first_gates.T, second_routes.T, second_gates.T, hidden_gain[None],
              embed_gain[None])
    scratch += [pltpu.VMEM(small.shape, small.dtype) for small in smalls]
    return pl.pallas_call(
        functools.partial(block_kernel, devices),
        out_shape=jax.ShapeDtypeStruct((tok, width), bf16),
        in_specs=[hbm] * 13,
        out_specs=hbm,
        scratch_shapes=scratch,
        compiler_params=pltpu.CompilerParams(
            collective_id=0, has_side_effects=True, vmem_limit_bytes=VMEM_LIMIT
        ),
    )(*smalls, hidden_rows, token_embed, first_gate_up, first_down, merge_weight,
      second_gate_up, second_down)


def rms_scale(values, gain_vec):
    widened = values.astype(jnp.float32)
    inverse_rms = lax.rsqrt(jnp.mean(widened * widened, axis=-1, keepdims=True) + EPSILON)
    return (widened * inverse_rms * gain_vec).astype(jnp.bfloat16)


def dense_gates(routes, gates, experts):
    hit = routes[:, :, None] == jnp.arange(experts, dtype=jnp.int32)[None, None, :]
    return jnp.sum(jnp.where(hit, gates[:, :, None], 0.0), axis=1)


def plain_layer(devices, rows, routes, gates, gate_up, down):
    dense = lax.all_gather(dense_gates(routes, gates, devices), "inner", axis=0, tiled=True)
    column = lax.dynamic_slice_in_dim(dense, lax.axis_index("inner"), 1, axis=1)
    everyone = lax.all_gather(rows, "inner", axis=0, tiled=True)
    width = down.shape[1]
    projected = jnp.dot(everyone, gate_up[0], preferred_element_type=jnp.float32)
    inner = narrow(jax.nn.silu(projected[:, :width]) * projected[:, width:])
    share = narrow(jnp.dot(inner, down[0], preferred_element_type=jnp.float32) * column)
    total = lax.psum_scatter(share, "inner", scatter_dimension=0, tiled=True)
    return narrow(wide(rows) + wide(total))


def plain_merge(after_first, merged_in, weight):
    columns = lax.all_to_all(merged_in, "inner", split_axis=1, concat_axis=0, tiled=True)
    partial = narrow(jnp.dot(columns, weight, preferred_element_type=jnp.float32))
    merged = lax.psum_scatter(partial, "inner", scatter_dimension=0, tiled=True)
    return narrow(wide(after_first) + jax.nn.silu(wide(merged)))


def unfused(hidden_rows, token_embed, first_routes, first_gates, first_gate_up, first_down,
            second_routes, second_gates, second_gate_up, second_down, hidden_gain, embed_gain,
            merge_weight):
    devices = lax.axis_size("inner")
    after_first = plain_layer(
        devices, hidden_rows, first_routes, first_gates, first_gate_up, first_down
    )
    merged_in = jnp.concatenate(
        [rms_scale(after_first, hidden_gain), rms_scale(token_embed, embed_gain)], axis=1
    )
    after_merge = plain_merge(after_first, merged_in, merge_weight)
    return plain_layer(devices, after_merge, second_routes, second_gates, second_gate_up, second_down)


def local(hidden_rows, *others):
    devices = lax.axis_size("inner")
    tok, width = hidden_rows.shape
    fits = (
        12 * devices * tok * width * 2 <= VMEM_LIMIT
        and devices % 4 == 0 and devices >= 16 and tok % 32 == 0 and width % (CUTS * LANES) == 0
    )
    return (fused if fits else unfused)(hidden_rows, *others)


def solution(mesh):
    rows = P(("groups", "inner"), None)
    return jax.shard_map(
        local,
        mesh=mesh,
        in_specs=(
            rows, rows, rows, rows,
            P("inner", None, None),
            P("inner", None, None),
            rows, rows,
            P("inner", None, None),
            P("inner", None, None),
            P(),
            P(),
            P("inner", None),
        ),
        out_specs=rows,
        check_vma=False,
    )
```

```python
import functools

import jax
import jax.numpy as jnp
from jax import lax
from jax.experimental import pallas as pl
from jax.experimental.pallas import tpu as pltpu
from jax.sharding import PartitionSpec as P

EPSILON = 1e-06
LANES = 128
CUTS = 4
VMEM_LIMIT = 60 * 1024 * 1024


class Ring:
    def __init__(self, devices, tok):
        self.devices, self.tok = devices, tok
        self.chips = devices // 2
        self.reach = self.chips // 2
        self.rise = self.chips // 2
        me = lax.axis_index("inner")
        chip = me // 2
        across = chip % 2
        along = chip // 2
        self.core = me % 2
        self.place = along * (1 - across) + (2 * self.rise - 1 - along) * across
        self.me = me
        self.spans = [(0, 0)]
        for distance in range(1, self.reach):
            self.spans += [(distance, 0), (distance, 1)]
        self.spans.append((self.reach, 0))

    def device(self, shift, other):
        place = (self.place + shift + self.chips) % self.chips
        across = place // self.rise
        along = place * (1 - across) + (2 * self.rise - 1 - place) * across
        core = self.core * (1 - other) + (1 - self.core) * other
        return (along * 2 + across) * 2 + core

    def first(self, distance, s):
        if distance == 0:
            return ((self.reach - 1) * 4 + 2) * self.tok
        return ((distance - 1) * 4 + 2 * s) * self.tok

    def rows(self, distance, s):
        return pl.ds(self.first(distance, s), 2 * self.tok)

    def side(self, distance, s, other):
        return pl.ds(self.first(distance, s) + other * self.tok, self.tok)

    def half(self, way, distance, other, k):
        part = self.tok // 2
        if distance == 0:
            s, column = 0, k
        elif distance == self.reach:
            s, column = 0, k
        else:
            s, column = (0 if k == way else 1), way
        return pl.ds(self.first(distance, s) + other * self.tok + column * part, part)

    def chunk(self, way, distance, k):
        if distance == self.reach:
            return way
        return 2 + (way * (self.reach - 1) + distance - 1) * 2 + k

    def slot(self, way, distance, other):
        if distance == 0:
            return (self.reach - 1) * 4 + 2 + other
        if distance == self.reach:
            return (self.reach - 1) * 4 + other
        return (distance - 1) * 4 + way * 2 + other


def remote(src, dst, send, recv, device):
    return pltpu.make_async_remote_copy(
        src_ref=src, dst_ref=dst, send_sem=send, recv_sem=recv,
        device_id={"inner": device}, device_id_type=pl.DeviceIdType.MESH,
    )


def wide(values):
    return values.astype(jnp.float32)


def narrow(values):
    return values.astype(jnp.bfloat16)


def sent(ring, whole, sem):
    remote(whole, whole, sem, sem, ring.device(0, 1)).wait_send()


class Reduce:
    def __init__(self, ring, bufs, recvs):
        self.ring = ring
        self.share, self.paired, self.arrived, self.send = bufs
        self.pair_recv, self.recv = recvs
        self.cut = self.share.shape[1] // CUTS

    def pair_copy(self, distance, s):
        ring = self.ring
        slot = ring.spans.index((distance, s))
        here = self.paired.at[pl.ds(slot * ring.tok, ring.tok)]
        return remote(
            self.share.at[ring.side(distance, s, 1)], here,
            self.send.at[0], self.pair_recv.at[slot], ring.device(0, 1),
        ), here

    def start_pair(self, distance, s):
        self.pair_copy(distance, s)[0].start()

    def finish_pair(self, distance, s):
        copy, here = self.pair_copy(distance, s)
        copy.wait_recv()
        rows = self.ring.side(distance, s, 0)
        self.share[rows, :] = narrow(wide(self.share[rows, :]) + wide(here[...]))

    def columns(self, c):
        return pl.ds(c * self.cut, self.cut)

    def far_copy(self, c):
        ring = self.ring
        slot = 2 * ring.reach - 1
        here = self.paired.at[pl.ds(slot * ring.tok, ring.tok), self.columns(c)]
        return remote(
            self.share.at[ring.side(ring.reach, 0, 1), self.columns(c)], here,
            self.send.at[0], self.pair_recv.at[slot + c], ring.device(0, 1),
        ), here

    def launch_far(self):
        ring = self.ring
        for c in range(CUTS):
            copy, here = self.far_copy(c)
            copy.wait_recv()
            at = (ring.side(ring.reach, 0, 0), self.columns(c))
            self.share[at] = narrow(wide(self.share[at]) + wide(here[...]))
            for way in (0, 1):
                self.hop(way, ring.reach, way, c)[0].start()

    def hop(self, way, distance, k, c):
        ring = self.ring
        rows = ring.tok // 2
        slot = ring.chunk(way, distance, k)
        landing = self.arrived.at[pl.ds(slot * rows, rows), self.columns(c)]
        return remote(
            self.share.at[ring.half(1 - way, distance, 0, k), self.columns(c)], landing,
            self.send.at[1], self.recv.at[slot * CUTS + c],
            ring.device(1 - 2 * way, 0),
        ), landing

    def launch(self, distance, flip):
        for c in range(CUTS):
            for way in (0, 1):
                self.hop(way, distance, 1 - way if flip else way, c)[0].start()

    def step(self, distance, flip, cuts=range(CUTS)):
        for c in cuts:
            for way in (0, 1):
                k = 1 - way if flip else way
                copy, landing = self.hop(way, distance + 1, k, c)
                copy.wait_recv()
                at = (self.ring.half(1 - way, distance, 0, k), self.columns(c))
                self.share[at] = narrow(wide(self.share[at]) + wide(landing[...]))
                self.hop(way, distance, k, c)[0].start()

    def drain(self):
        ring = self.ring
        sent(ring, self.share.at[pl.ds(0, 2 * ring.reach * ring.tok)], self.send.at[0])
        sent(ring, self.share.at[pl.ds(0, (2 * ring.reach - 1) * ring.tok)], self.send.at[1])

    def piece(self, c):
        halves = []
        for k in (0, 1):
            piece = wide(self.share[self.ring.half(0, 0, 0, k), self.columns(c)])
            for way in (0, 1):
                copy, landing = self.hop(way, 1, k, c)
                copy.wait_recv()
                piece = piece + wide(landing[...])
            halves.append(piece)
        return jnp.concatenate(halves, axis=0)

    def total(self):
        return jnp.concatenate([self.piece(c) for c in range(CUTS)], axis=1)


def reduce_scratch(devices, tok, width):
    reach = devices // 4
    return [
        pltpu.VMEM((devices * tok, width), jnp.bfloat16),
        pltpu.VMEM((2 * reach * tok, width), jnp.bfloat16),
        pltpu.VMEM(((2 * reach - 1) * tok, width), jnp.bfloat16),
        pltpu.SemaphoreType.DMA((2,)),
    ]


def reduce_recvs(devices):
    reach = devices // 4
    return [
        pltpu.SemaphoreType.DMA((2 * reach - 1 + CUTS,)),
        pltpu.SemaphoreType.DMA(((4 * reach - 2) * CUTS,)),
    ]


def gather_scratch(devices, tok, width):
    return [
        pltpu.VMEM((devices * tok, width), jnp.bfloat16),
        pltpu.SemaphoreType.DMA((2,)),
    ]


def normed(values, gain):
    widened = wide(values)
    inverse_rms = lax.rsqrt(jnp.mean(widened * widened, axis=-1, keepdims=True) + EPSILON)
    return narrow(widened * inverse_rms * gain)


def gate_lanes(devices, turned, tables):
    rows = tables[0][0].shape[1]
    turned[...] = jnp.zeros_like(turned)
    for layer, (routes, gates) in enumerate(tables):
        base = 2 * layer * devices
        expert = lax.broadcasted_iota(jnp.int32, (devices, rows), 0)
        dense = jnp.zeros((devices, rows), jnp.float32)
        for k in range(routes.shape[0]):
            dense = dense + jnp.where(expert == routes[k : k + 1, :], gates[k : k + 1, :], 0.0)
        high = wide(narrow(dense))
        turned[base : base + devices, :rows] = high
        turned[base + devices : base + 2 * devices, :rows] = dense - high
    return narrow(turned[...].T[:rows, :])


def block_kernel(devices, *refs):
    smalls = refs[:6]
    hidden_ref, embed_ref, gu1_ref, down1_ref, weight_ref, gu2_ref, down2_ref, out_ref = refs[6:14]
    scratch = list(refs[14:])
    take = lambda count: [scratch.pop(0) for _ in range(count)]
    gu1, down1, weight, gu2, down2, load_sem = take(6)
    turned, embed, after_first, pieces, landed, inner = take(6)
    piece_send, piece_recv, own_sem, ring_recv, sib_recv = take(5)
    gather1, gather2 = take(2), take(2)
    reduce1, reduce2, reduce3 = take(4), take(4), take(4)
    recvs1, recvs2 = take(2), take(2)
    out, out_sem = take(2)
    routes1, gates1, routes2, gates2, hidden_gain, embed_gain = held = take(6)
    tok, width = hidden_ref.shape
    hidden = down1.shape[0]
    depth = weight.shape[0]
    lanes = gather1[0].shape[1] - width
    ring = Ring(devices, tok)
    reach = ring.reach
    part = tok // 2

    barrier = pltpu.get_barrier_semaphore()
    neighbours = [ring.device(1, 0), ring.device(-1, 0), ring.device(0, 1)]
    for device in neighbours:
        pl.semaphore_signal(
            barrier, inc=1, device_id={"inner": device}, device_id_type=pl.DeviceIdType.MESH
        )
    own_rows = ring.side(0, 0, 0)
    loads = [
        pltpu.make_async_copy(source, target, load_sem.at[i])
        for i, (source, target) in enumerate(
            [(hidden_ref, gather1[0].at[own_rows, pl.ds(0, width)]), (embed_ref, embed),
             (gu1_ref.at[0], gu1), (down1_ref.at[0], down1), (weight_ref, weight),
             (gu2_ref.at[0], gu2), (down2_ref.at[0], down2), *zip(smalls, held)]
        )
    ]
    for load in loads[7:] + loads[:7]:
        load.start()
    waiting = list(range(len(loads)))

    def need(*which):
        for i in which:
            if i in waiting:
                waiting.remove(i)
                loads[i].wait()

    def begin(copy):
        copy.start()

    partners = [(0, 0, 1)]
    for distance in range(1, reach + 1):
        for other in (0, 1):
            partners.append((0, distance, other))
            if distance < reach:
                partners.append((1, distance, other))

    def streams(s):
        return [(way, 1 - way if s else way) for way in (0, 1)]

    def ring_copy(bufs, way, distance, k, cut=None):
        everyone, send = bufs
        slot = ring.chunk(way, distance, k)
        rows = ring.half(way, max(distance - 1, 0), 0, k)
        landing = ring.half(way, distance, 0, k)
        cut = pl.ds(0, everyone.shape[1]) if cut is None else cut
        return remote(
            everyone.at[rows, cut], everyone.at[landing, cut], send.at[0], ring_recv.at[slot],
            ring.device(1 - 2 * way, 0),
        )

    def sibling_copy(bufs, way, distance, k):
        everyone, send = bufs
        if distance == 0:
            s, origin, landing = 0, own_rows, ring.side(0, 0, 1)
        else:
            s = 0 if distance == reach or k == way else 1
            origin, landing = ring.half(way, distance, 0, k), ring.half(way, distance, 1, k)
        return remote(
            everyone.at[origin], everyone.at[landing], send.at[1],
            sib_recv.at[ring.spans.index((distance, s))], ring.device(0, 1),
        )

    def first_sends():
        everyone, send = gather1
        narrow_cut, lane_cut = pl.ds(0, width), pl.ds(width, lanes)

        def send_rows(way, k):
            return remote(
                hidden_ref.at[pl.ds(k * part, part)],
                everyone.at[ring.half(way, 1, 0, k), narrow_cut],
                send.at[0], ring_recv.at[ring.chunk(way, 1, k)], ring.device(1 - 2 * way, 0),
            )

        def send_lanes(way, k):
            return remote(
                everyone.at[ring.half(way, 0, 0, k), lane_cut],
                everyone.at[ring.half(way, 1, 0, k), lane_cut],
                send.at[0], ring_recv.at[ring.chunk(way, 1, k)], ring.device(1 - 2 * way, 0),
            )

        need(*range(7, len(loads)))
        everyone[own_rows, lane_cut] = gate_lanes(
            devices, turned, [(routes1[...], gates1[...]), (routes2[...], gates2[...])]
        )
        pl.semaphore_wait(barrier, len(neighbours))
        for way, k in streams(0):
            begin(send_rows(way, k))
            begin(send_lanes(way, k))
        begin(remote(
            hidden_ref, everyone.at[ring.side(0, 0, 1), narrow_cut],
            send.at[1], sib_recv.at[0], ring.device(0, 1),
        ))
        begin(remote(
            everyone.at[own_rows, lane_cut], everyone.at[ring.side(0, 0, 1), lane_cut],
            send.at[1], sib_recv.at[0], ring.device(0, 1),
        ))
        for way, k in streams(1):
            begin(send_rows(way, k))
            begin(send_lanes(way, k))

    def layer(bufs, first, reducing, load_ids, gu, down, meanwhile):
        everyone = bufs[0]
        share = reducing.share
        gate_rows = gather1[0]
        step = min(256, hidden)
        steps = hidden // step

        def pass_on(distance, s):
            for way, k in streams(s):
                ring_copy(bufs, way, distance, k).wait_recv()
                if distance + 1 < reach or (distance + 1 == reach and s == 0):
                    begin(ring_copy(bufs, way, distance + 1, k))
            for way, k in streams(s):
                begin(sibling_copy(bufs, way, distance, k))

        def from_sibling(distance, s):
            both = bufs[0].at[ring.side(distance, s, 1)]
            remote(
                both, both, bufs[1].at[1], sib_recv.at[ring.spans.index((distance, s))],
                ring.device(0, 1),
            ).wait_recv()

        def up(first_row, count, low, high):
            rows = pl.ds(first_row, count)

            for j in range(low, high):
                left, right = pl.ds(j * step, step), pl.ds(hidden + j * step, step)
                x = everyone[rows, :width]
                g = jnp.dot(x, gu[:, left], preferred_element_type=jnp.float32)
                u = jnp.dot(x, gu[:, right], preferred_element_type=jnp.float32)
                inner[:count, left] = narrow(jax.nn.silu(g) * u)

        def finish(span):
            count = 2 * tok
            rows = ring.rows(*span)
            lane = lax.broadcasted_iota(jnp.int32, (count, lanes), 1)
            mine = (lane == ring.me + first * devices) | (lane == ring.me + (first + 1) * devices)
            gate = jnp.sum(
                jnp.where(mine, wide(gate_rows[rows, width:]), 0.0), axis=1, keepdims=True
            )
            for c in range(CUTS):
                cut = reducing.columns(c)
                out = jnp.dot(
                    inner[:count, :], down[:, cut], preferred_element_type=jnp.float32
                )
                share[rows, cut] = narrow(out * gate)
                if span == (reach, 0):
                    reducing.far_copy(c)[0].start()

            if span != (reach, 0):
                reducing.start_pair(*span)

        last = reach - 1
        spans = ring.spans
        from_sibling(0, 0)
        need(load_ids[0])
        up(ring.first(0, 0), 2 * tok, 0, steps)
        pass_on(1, 0)
        need(load_ids[1])
        finish((0, 0))
        meanwhile()
        for at, span in enumerate(spans[1:-1], 1):
            if span == (last, 1):
                reducing.finish_pair(last, 0)
                reducing.launch(last, True)
            from_sibling(*span)
            up(ring.first(*span), 2 * tok, 0, steps)
            pass_on(*spans[at + 1])
            finish(span)
            if span != (last, 1):
                reducing.finish_pair(*spans[at - 1])
        from_sibling(reach, 0)
        up(ring.first(reach, 0), 2 * tok, 0, steps // 2)
        reducing.step(last - 1, True, range(0, 1))
        up(ring.first(reach, 0), 2 * tok, steps // 2, steps)
        reducing.step(last - 1, True, range(1, CUTS - 1))
        finish((reach, 0))
        reducing.step(last - 1, True, range(CUTS - 1, CUTS))
        reducing.launch_far()
        reducing.finish_pair(last, 1)
        for distance in range(last, 0, -1):
            if distance > 2:
                reducing.step(distance - 2, True)
            reducing.step(distance, False)

    def target_of(way, distance, other):
        return ring.device(distance * (1 - 2 * way), other)

    def piece(way, distance, other):
        target = target_of(way, distance, other)
        slot = ring.slot(way, distance, other)
        return remote(
            pieces.at[target], landed.at[pl.ds(slot * tok, tok)],
            piece_send.at[0], piece_recv.at[distance], target,
        )

    def send_pieces():
        for partner in reversed(partners):
            begin(piece(*partner))

    def merge(reducing):
        own = pltpu.make_async_copy(
            pieces.at[ring.me], landed.at[pl.ds(ring.slot(0, 0, 0) * tok, tok)], own_sem.at[0]
        )
        own.start()
        need(4)
        share = reducing.share
        came = set()

        def arrive(distance):
            if distance not in came:
                came.add(distance)
                low = min(ring.slot(*p) for p in partners if p[1] == distance)
                count = sum(p[1] == distance for p in partners)
                whole = landed.at[pl.ds(low * tok, count * tok)]
                remote(
                    whole, whole, piece_send.at[0], piece_recv.at[distance], ring.device(0, 1)
                ).wait_recv()
                if distance == 0:
                    own.wait()

        def product(distance, s):
            arrive(distance)
            pick = []
            for other in (0, 1):
                for column in (0, 1):
                    if distance in (0, reach):
                        way, k = 0, column
                    else:
                        way, k = column, (column if s == 0 else 1 - column)
                    row = ring.slot(way, distance, other) * tok + k * part
                    pick.append(landed[row : row + part, :])
            x = jnp.concatenate(pick, axis=0)
            rows = ring.rows(distance, s)
            for c in range(CUTS):
                cut = reducing.columns(c)
                share[rows, cut] = narrow(
                    jnp.dot(x, weight[:, cut], preferred_element_type=jnp.float32)
                )
                if distance == reach:
                    reducing.far_copy(c)[0].start()
            if distance != reach:
                reducing.start_pair(distance, s)

        last = reach - 1
        product(reach, 0)
        product(last, 0)
        reducing.launch_far()
        product(last, 1)
        reducing.finish_pair(last, 0)
        reducing.launch(last, True)
        product(last - 1, 0)
        reducing.finish_pair(last, 1)
        for distance in range(last, 0, -1):
            if distance > 1:
                product(distance - 1, 1)
                reducing.finish_pair(distance - 1, 0)
            else:
                product(0, 0)
            reducing.step(distance, False)
            if distance > 1:
                if distance > 2:
                    product(distance - 2, 0)
                reducing.finish_pair(distance - 1, 1)
                reducing.step(distance - 1, True)
        reducing.finish_pair(0, 0)

    def scatter_pieces(values, at):
        for j in range(width // depth):
            pieces[at + j] = values[:, j * depth : (j + 1) * depth]

    def embed_pieces():
        need(1)
        scatter_pieces(normed(embed[...], embed_gain[...]), width // depth)

    first_sends()
    need(0)
    reducing1 = reducing = Reduce(ring, reduce1, recvs1)
    layer(gather1, 0, reducing, (2, 3), gu1, down1, embed_pieces)
    squares = jnp.zeros((tok, 1), jnp.float32)
    for c in range(CUTS):
        cut = reducing.columns(c)
        first = narrow(wide(gather1[0][own_rows, cut]) + reducing.piece(c))
        after_first[:, cut] = first
        squares = squares + jnp.sum(wide(first) * wide(first), axis=-1, keepdims=True)
    inverse_rms = lax.rsqrt(squares / width + EPSILON)
    for j in range(width // depth):
        cut = pl.ds(j * depth, depth)
        pieces[j] = narrow(wide(after_first[:, cut]) * inverse_rms * hidden_gain[:, cut])
    send_pieces()
    reducing2 = reducing = Reduce(ring, reduce2, recvs2)
    merge(reducing)
    everyone, send = gather2
    for c in range(CUTS):
        cut = reducing.columns(c)
        everyone[own_rows, cut] = narrow(
            wide(after_first[:, cut]) + jax.nn.silu(reducing.piece(c))
        )
        for way, k in streams(0):
            begin(ring_copy(gather2, way, 1, k, cut))
    for way, k in streams(1):
        begin(ring_copy(gather2, way, 1, k))
    begin(sibling_copy(gather2, 0, 0, 0))
    reducing3 = reducing = Reduce(ring, reduce3, recvs2)
    layer(gather2, 2, reducing, (5, 6), gu2, down2, lambda: None)
    stores = []
    for c in range(CUTS):
        cut = reducing.columns(c)
        out[:, cut] = narrow(wide(gather2[0][own_rows, cut]) + reducing.piece(c))
        stores.append(pltpu.make_async_copy(out.at[:, cut], out_ref.at[:, cut], out_sem.at[c]))
        stores[-1].start()
    for everyone, send in (gather1, gather2):
        sent(ring, everyone.at[pl.ds(0, (2 * reach - 1) * tok)], send.at[0])
        sent(ring, everyone.at[pl.ds(0, 2 * reach * tok)], send.at[1])
    sent(ring, landed.at[pl.ds(0, (devices - 1) * tok)], piece_send.at[0])
    for each in (reducing1, reducing2, reducing3):
        each.drain()
    for store in stores:
        store.wait()


def fused(hidden_rows, token_embed, first_routes, first_gates, first_gate_up, first_down,
          second_routes, second_gates, second_gate_up, second_down, hidden_gain, embed_gain,
          merge_weight):
    devices = lax.axis_size("inner")
    tok, width = hidden_rows.shape
    hidden = first_down.shape[1]
    depth = merge_weight.shape[0]
    lanes = -(-4 * devices // LANES) * LANES
    reach = devices // 4
    hbm = pl.BlockSpec(memory_space=pl.ANY)
    bf16 = jnp.bfloat16
    scratch = [
        pltpu.VMEM(first_gate_up.shape[1:], bf16),
        pltpu.VMEM(first_down.shape[1:], bf16),
        pltpu.VMEM(merge_weight.shape, bf16),
        pltpu.VMEM(second_gate_up.shape[1:], bf16),
        pltpu.VMEM(second_down.shape[1:], bf16),
        pltpu.SemaphoreType.DMA((13,)),
        pltpu.VMEM((lanes, -(-tok // LANES) * LANES), jnp.float32),
        pltpu.VMEM((tok, width), bf16),
        pltpu.VMEM((tok, width), bf16),
        pltpu.VMEM((devices, tok, depth), bf16),
        pltpu.VMEM((devices * tok, depth), bf16),
        pltpu.VMEM((4 * tok, hidden), bf16),
        pltpu.SemaphoreType.DMA((1,)),
        pltpu.SemaphoreType.DMA((reach + 1,)),
        pltpu.SemaphoreType.DMA((1,)),
        pltpu.SemaphoreType.DMA((4 * reach - 2,)),
        pltpu.SemaphoreType.DMA((2 * reach,)),
    ]
    scratch += gather_scratch(devices, tok, width + lanes) + gather_scratch(devices, tok, width)
    for _ in range(3):
        scratch += reduce_scratch(devices, tok, width)
    scratch += reduce_recvs(devices) + reduce_recvs(devices)
    scratch += [pltpu.VMEM((tok, width), bf16), pltpu.SemaphoreType.DMA((CUTS,))]
    smalls = (first_routes.T, first_gates.T, second_routes.T, second_gates.T, hidden_gain[None],
              embed_gain[None])
    scratch += [pltpu.VMEM(small.shape, small.dtype) for small in smalls]
    return pl.pallas_call(
        functools.partial(block_kernel, devices),
        out_shape=jax.ShapeDtypeStruct((tok, width), bf16),
        in_specs=[hbm] * 13,
        out_specs=hbm,
        scratch_shapes=scratch,
        compiler_params=pltpu.CompilerParams(
            collective_id=0, has_side_effects=True, vmem_limit_bytes=VMEM_LIMIT
        ),
    )(*smalls, hidden_rows, token_embed, first_gate_up, first_down, merge_weight,
      second_gate_up, second_down)


def rms_scale(values, gain_vec):
    widened = values.astype(jnp.float32)
    inverse_rms = lax.rsqrt(jnp.mean(widened * widened, axis=-1, keepdims=True) + EPSILON)
    return (widened * inverse_rms * gain_vec).astype(jnp.bfloat16)


def dense_gates(routes, gates, experts):
    hit = routes[:, :, None] == jnp.arange(experts, dtype=jnp.int32)[None, None, :]
    return jnp.sum(jnp.where(hit, gates[:, :, None], 0.0), axis=1)


def plain_layer(devices, rows, routes, gates, gate_up, down):
    dense = lax.all_gather(dense_gates(routes, gates, devices), "inner", axis=0, tiled=True)
    column = lax.dynamic_slice_in_dim(dense, lax.axis_index("inner"), 1, axis=1)
    everyone = lax.all_gather(rows, "inner", axis=0, tiled=True)
    width = down.shape[1]
    projected = jnp.dot(everyone, gate_up[0], preferred_element_type=jnp.float32)
    inner = narrow(jax.nn.silu(projected[:, :width]) * projected[:, width:])
    share = narrow(jnp.dot(inner, down[0], preferred_element_type=jnp.float32) * column)
    total = lax.psum_scatter(share, "inner", scatter_dimension=0, tiled=True)
    return narrow(wide(rows) + wide(total))


def plain_merge(after_first, merged_in, weight):
    columns = lax.all_to_all(merged_in, "inner", split_axis=1, concat_axis=0, tiled=True)
    partial = narrow(jnp.dot(columns, weight, preferred_element_type=jnp.float32))
    merged = lax.psum_scatter(partial, "inner", scatter_dimension=0, tiled=True)
    return narrow(wide(after_first) + jax.nn.silu(wide(merged)))


def unfused(hidden_rows, token_embed, first_routes, first_gates, first_gate_up, first_down,
            second_routes, second_gates, second_gate_up, second_down, hidden_gain, embed_gain,
            merge_weight):
    devices = lax.axis_size("inner")
    after_first = plain_layer(
        devices, hidden_rows, first_routes, first_gates, first_gate_up, first_down
    )
    merged_in = jnp.concatenate(
        [rms_scale(after_first, hidden_gain), rms_scale(token_embed, embed_gain)], axis=1
    )
    after_merge = plain_merge(after_first, merged_in, merge_weight)
    return plain_layer(devices, after_merge, second_routes, second_gates, second_gate_up, second_down)


def local(hidden_rows, *others):
    devices = lax.axis_size("inner")
    tok, width = hidden_rows.shape
    fits = (
        12 * devices * tok * width * 2 <= VMEM_LIMIT
        and devices % 4 == 0 and devices >= 16 and tok % 32 == 0 and width % (CUTS * LANES) == 0
    )
    return (fused if fits else unfused)(hidden_rows, *others)


def solution(mesh):
    rows = P(("groups", "inner"), None)
    return jax.shard_map(
        local,
        mesh=mesh,
        in_specs=(
            rows, rows, rows, rows,
            P("inner", None, None),
            P("inner", None, None),
            rows, rows,
            P("inner", None, None),
            P("inner", None, None),
            P(),
            P(),
            P("inner", None),
        ),
        out_specs=rows,
        check_vma=False,
    )
```
